32 devices in a mesh: groups: 2 (over x), seq: 16 (over z, y, core).
Axes of the slice: x: 2, y: 2, z: 4, core: 2. Of those that a mesh axis runs over, the one named last changes fastest.
Arguments:
- queries: bfloat16 [8192, 256], P(('groups', 'seq')), parts along dimension 0, may hold values from -10 to 10
- key_vectors: bfloat16 [8192, 256], P(('groups', 'seq')), parts along dimension 0, may hold values from -10 to 10
- value_vectors: bfloat16 [8192, 1024], P(('groups', 'seq')), parts along dimension 0, may hold values from -6 to 6
- output_grad: bfloat16 [8192, 1024], P(('groups', 'seq')), parts along dimension 0, may hold values from -6 to 6
- norm_gain: float32 [1024], replicated, may hold values from 0.5 to 1.5
Outputs:
- mixed_out: bfloat16 [8192, 1024], P(('groups', 'seq')), parts along dimension 0
- query_grad: bfloat16 [8192, 256], P(('groups', 'seq')), parts along dimension 0
- key_grad: bfloat16 [8192, 256], P(('groups', 'seq')), parts along dimension 0
- value_grad: bfloat16 [8192, 1024], P(('groups', 'seq')), parts along dimension 0
The draws below stay inside these ranges and needn't reach their ends.
There are 2 independent parts, one for each index of `groups`. The reference program is written for one: setup_inputs(seed, part) draws one part's arguments, and reference() takes and returns one part's arrays. A program takes and returns all parts, laid end to end along the dimension named above; an argument that names none is the same for every part. Nothing has to cross between parts.
All inputs are finite; a program needn't handle non-finite values.
Results may differ from the reference program's by a relative error of at most 0.017.
Values may be sent and summed in bfloat16 or wider, within the bound.
A program may use at most 128 MiB of HBM per device.

```python
import jax
import jax.numpy as jnp
from jax import lax

H = 16
FD = 16
DV = 64
WIN = 64
BLK = 256
FEAT = 273
TOKENS = 4096


def paired_vectors(key, part):
    base_key = jax.random.fold_in(key, 7)
    array_shape = (TOKENS, H * FD)
    query_out = jnp.clip(jax.random.normal(jax.random.fold_in(base_key, 1), array_shape, jnp.float32), -6.0, 6.0)
    key_out = jnp.clip(jax.random.normal(jax.random.fold_in(base_key, 2), array_shape, jnp.float32), -6.0, 6.0)
    return (query_out, key_out)


def draw_queries(key, part):
    return paired_vectors(key, part)[0].astype(jnp.bfloat16)


def draw_key_vectors(key, part):
    return paired_vectors(key, part)[1].astype(jnp.bfloat16)


def levels(own_key, shape, shards, smallest, high):
    gain = 1.0
    for dim, shards_of in shards:
        draws = jax.random.uniform(jax.random.fold_in(jax.random.fold_in(own_key, 6), dim), (shards_of,), jnp.float32, smallest / len(shards), high / len(shards))
        gain = gain * jnp.repeat(jnp.exp(draws), shape[dim] // shards_of).reshape((-1,) + (1,) * (len(shape) - 1 - dim))
    return gain


def noise(rng, extent, scale, bound, cuts=(), held_as=jnp.bfloat16):
    array = scale * jax.random.normal(rng, extent, jnp.float32)
    if cuts:
        array = array * levels(rng, extent, cuts, -0.22, 0.18)
    return jnp.clip(array, -bound, bound).astype(held_as)


def setup_inputs(seed: int = 0, part: int = 0) -> dict:
    splits = jax.random.split(jax.random.key(seed), 6)
    part_splits = jax.random.split(jax.random.fold_in(splits[5], part), 6)
    queries = draw_queries(jax.random.fold_in(jax.random.fold_in(splits[5], part), 71), part)
    key_vectors = draw_key_vectors(jax.random.fold_in(jax.random.fold_in(splits[5], part), 71), part)
    value_vectors = noise(part_splits[2], (TOKENS, H * DV), 1.0, 6.0, ((0, 16),))
    output_grad = noise(part_splits[3], (TOKENS, H * DV), 1.0, 6.0, ((0, 16),))
    norm_gain = jnp.clip(1.0 + 0.1 * jax.random.normal(splits[4], (H * DV,), jnp.float32), 0.5, 1.5)
    return {"queries": queries, "key_vectors": key_vectors, "value_vectors": value_vectors, "output_grad": output_grad, "norm_gain": norm_gain}


quad_scale = 0.17677669529663687
epsilon = 1e-06
masked_score = -1e+30

def taylor_features(vectors, packed):
    row_count, head_count, feature_width = vectors.shape
    pieces = [jnp.ones((row_count, head_count, 1), jnp.float32), vectors * 0.5]
    if packed:
        for column in range(feature_width):
            factor = jnp.where(jnp.arange(feature_width - column) == 0, quad_scale, 0.25).astype(jnp.float32)
            pieces.append(vectors[:, :, column:column + 1] * vectors[:, :, column:] * factor)
    else:
        outer_product = vectors[:, :, :, None] * vectors[:, :, None, :]
        pieces.append(outer_product.reshape(row_count, head_count, feature_width * feature_width) * quad_scale)
    return jnp.concatenate(pieces, axis=-1)

def block_state(key_block, value_block, packed):
    row_count = key_block.shape[0]
    features = taylor_features(key_block.reshape(row_count, H, FD), packed)
    state_out = jnp.einsum('thf,the->fhe', features, value_block.reshape(row_count, H, DV), precision=lax.Precision.HIGHEST)
    return state_out.reshape(features.shape[-1], H * DV)

def mix_block(query_block, key_window, value_window, state_in, norm_gain, first_block):
    row_count = query_block.shape[0]
    key_span = key_window.shape[0]
    lookback = key_span - row_count
    packed = state_in.shape[0] != FEAT
    query_heads = query_block.reshape(row_count, H, FD)
    key_heads = key_window.reshape(key_span, H, FD)
    value_heads = value_window.reshape(key_span, H, DV)
    remote = jnp.einsum('thf,fhe->the', taylor_features(query_heads, packed), state_in.reshape(state_in.shape[0], H, DV), precision=lax.Precision.HIGHEST)
    query_half = query_heads.astype(jnp.bfloat16)
    key_half = key_heads.astype(jnp.bfloat16)
    value_half = value_heads.astype(jnp.bfloat16)
    scores = jnp.einsum('thd,uhd->htu', query_half, key_half, preferred_element_type=jnp.float32) * 0.25
    row_index = jnp.arange(row_count)[:, None]
    col_index = jnp.arange(key_span)[None, :]
    same_block = (col_index >= lookback) & (col_index - lookback <= row_index)
    kernel = jnp.where(same_block, 1.0 + scores + 0.5 * scores * scores, 0.0).astype(jnp.bfloat16)
    local_sum = jnp.einsum('htu,uhe->the', kernel, value_half, preferred_element_type=jnp.float32)
    numerator = remote + local_sum
    inverse_rms = lax.rsqrt(lax.optimization_barrier(jnp.mean(numerator * numerator, axis=-1, keepdims=True)) + epsilon)
    linear = numerator * inverse_rms * norm_gain.reshape(H, DV)
    inside = (col_index > row_index) & (col_index <= row_index + lookback) & jnp.logical_or(col_index >= lookback, jnp.logical_not(first_block))
    masked = jnp.where(inside, scores, masked_score)
    row_peak = lax.stop_gradient(lax.optimization_barrier(jnp.max(masked, axis=-1, keepdims=True)))
    weights = jnp.exp(masked - row_peak)
    weights_half = (weights / lax.optimization_barrier(jnp.sum(weights, axis=-1, keepdims=True))).astype(jnp.bfloat16)
    attended = jnp.einsum('htu,uhe->the', weights_half, value_half, preferred_element_type=jnp.float32)
    return (linear + attended).reshape(row_count, H * DV).astype(jnp.bfloat16)

def forward(query_full, key_full, value_full, norm_gain):
    blocks = TOKENS // BLK
    key_blocks = key_full.reshape(blocks, BLK, H * FD)
    value_blocks = value_full.reshape(blocks, BLK, H * DV)
    states = lax.map(jax.checkpoint(lambda operands: block_state(operands[0], operands[1], False)), (key_blocks, value_blocks))
    totals = jnp.cumsum(states, axis=0)
    prefixes = jnp.concatenate([jnp.zeros_like(states[:1]), totals[:-1]], axis=0)
    key_extended = jnp.concatenate([jnp.zeros((WIN, H * FD), jnp.float32), key_full], axis=0)
    value_extended = jnp.concatenate([jnp.zeros((WIN, H * DV), jnp.float32), value_full], axis=0)

    def one_block(operands):
        block_index, query_block, prefix = operands
        start = (block_index * BLK).astype(jnp.int32)
        key_window = lax.dynamic_slice_in_dim(key_extended, start, BLK + WIN, 0)
        value_window = lax.dynamic_slice_in_dim(value_extended, start, BLK + WIN, 0)
        return mix_block(query_block, key_window, value_window, prefix, norm_gain, block_index == 0)
    outputs = lax.map(jax.checkpoint(one_block), (jnp.arange(blocks, dtype=jnp.int32), query_full.reshape(blocks, BLK, H * FD), prefixes))
    return outputs.reshape(TOKENS, H * DV)

def reference(queries, key_vectors, value_vectors, output_grad, norm_gain):
    query_full = queries.astype(jnp.float32)
    key_full = key_vectors.astype(jnp.float32)
    value_full = value_vectors.astype(jnp.float32)
    mixed_out, pullback = jax.vjp(lambda first_arg, second_arg, third_arg: forward(first_arg, second_arg, third_arg, norm_gain), query_full, key_full, value_full)
    query_grad, key_grad, value_grad = pullback(output_grad)
    return (mixed_out, query_grad.astype(jnp.bfloat16), key_grad.astype(jnp.bfloat16), value_grad.astype(jnp.bfloat16))
```

```python
import functools

import jax
import jax.numpy as jnp
from jax import lax
from jax.experimental import pallas as pl
from jax.experimental.pallas import tpu as pltpu
from jax.sharding import PartitionSpec as P

H = 16
FD = 16
DV = 64
WIN = 64
BLK = 256
LANES = 128
HC = H // 2
QW = HC * FD
VW = HC * DV
PACKED = VW + VW // 4
QUAD = 0.17677669529663687
EPS = 1e-06
NEG = -1e30
F32 = jnp.float32
BF16 = jnp.bfloat16

NN = (((1,), (0,)), ((), ()))
NT = (((1,), (1,)), ((), ()))
TN = (((0,), (0,)), ((), ()))


def mm(a, b, dims=NN):
    return lax.dot_general(a, b, dims, preferred_element_type=F32)


def features(x):
    parts = [x * x * QUAD]
    for d in range(1, 8):
        parts.append(x * pltpu.roll(x, FD - d, 0) * 0.25)
    parts.append(x[:8] * x[8:] * 0.25)
    row = lax.broadcasted_iota(jnp.int32, (8, x.shape[1]), 0)
    parts.append(jnp.where(row == 0, 1.0, 0.0).astype(F32))
    parts.append(x * 0.5)
    return jnp.concatenate(parts, axis=0).astype(BF16)


def features_back(g, x):
    dx = (2.0 * QUAD) * g[:FD] * x
    for d in range(1, 8):
        part = g[d * FD : (d + 1) * FD] * 0.25
        dx = dx + part * pltpu.roll(x, FD - d, 0) + pltpu.roll(part * x, d, 0)
    half = g[128:136] * 0.25
    dx = dx + jnp.concatenate([half * x[8:], half * x[:8]], axis=0)
    return dx + 0.5 * g[144:160]


def turn(dst, src):
    for c in range(src.shape[1] // LANES):
        cols = slice(c * LANES, (c + 1) * LANES)
        dst[cols, :] = src[:, cols].T


def put_state(buf, group, states):
    for i, st in enumerate(states):
        at = group * 256 + i * 64
        buf[at : at + 64, :] = st[:, :128].astype(BF16)
    rest = jnp.concatenate([st[:, 128:160] for st in states], axis=1)
    buf[VW + group * 64 : VW + group * 64 + 64, :] = rest.astype(BF16)


def get_state(buf, group, i):
    at = group * 256 + i * 64
    main = buf[at : at + 64, :]
    rest = buf[VW + group * 64 : VW + group * 64 + 64, :][:, i * 32 : (i + 1) * 32]
    return main, rest


def qk_rows(h):
    return pl.ds(pl.multiple_of(h * FD, FD), FD) if not isinstance(h, int) else slice(h * FD, (h + 1) * FD)


def v_rows(h):
    return pl.ds(pl.multiple_of(h * DV, DV), DV) if not isinstance(h, int) else slice(h * DV, (h + 1) * DV)


def head_mask(rows, width, which):
    row = lax.broadcasted_iota(jnp.int32, (128, rows), 0)
    return (row >= which * width) & (row < (which + 1) * width)


def tile_scores(kx, q_all, head):
    zero = jnp.zeros_like(q_all)
    picked = jnp.where(head_mask(LANES, FD, head), q_all, zero)
    return mm(kx, picked) * 0.25


def kernel_mask():
    r = lax.broadcasted_iota(jnp.int32, (128, 128), 0)
    c = lax.broadcasted_iota(jnp.int32, (128, 128), 1)
    return r <= c


def stage_state(kt, vt, state):
    for group in range(HC // 4):
        states = []
        for i in range(4):
            h = group * 4 + i
            phi = features(kt[qk_rows(h), :].astype(F32))
            states.append(mm(vt[v_rows(h), :], phi, NT))
        put_state(state, group, states)


def stage_local(first, qt_ref, dot_ref, num_ref, win_ref, dq_ref, dk_ref, dv_ref, kx, vx, ktx, vtx):
    r = lax.broadcasted_iota(jnp.int32, (192, 128), 0)
    c = lax.broadcasted_iota(jnp.int32, (192, 128), 1)
    band = (r >= c + 1) & (r <= c + 64)
    band0 = band if first is None else band & (r >= jnp.where(first, 64, 0))
    below = kernel_mask()

    @pl.loop(0, HC // 2)
    def _(pair):
        prow = pl.ds(pl.multiple_of(pair * LANES, LANES), LANES)
        for i in range(2):
            h = pair * 2 + i
            dks = []
            dvs = []
            for j in range(2):
                cols = slice(j * 128, (j + 1) * 128)
                keys = slice(j * 128, j * 128 + 256)
                s = tile_scores(kx[keys, :], qt_ref[:, cols], h)
                kern = 1.0 + s + 0.5 * s * s
                last = jnp.where(below, kern[128:], 0.0).astype(BF16)
                if j == 0:
                    local = mm(vtx[v_rows(h), 128:256], last)
                else:
                    local = mm(vtx[v_rows(h), 128:384],
                               jnp.concatenate([kern[:128].astype(BF16), last], axis=0))
                num_ref[v_rows(h), cols] = local
                sw = jnp.where(band0 if j == 0 else band, s[64:], NEG)
                e = jnp.exp(sw - jnp.max(sw, axis=0, keepdims=True))
                p = e * (1.0 / jnp.sum(e, axis=0, keepdims=True))
                w = p.astype(BF16)
                pad = jnp.zeros((64, 128), BF16)
                wide = jnp.concatenate([pad, w], axis=0)
                win_ref[v_rows(h), cols] = mm(vtx[v_rows(h), keys], wide)
                do_pair = dot_ref[prow, cols]
                do_one = jnp.where(head_mask(LANES, DV, i), do_pair, jnp.zeros_like(do_pair))
                vpair = vx[j * 128 + 64 : j * 128 + 256, prow]
                dw = mm(vpair, do_one)
                ds = p * (dw - jnp.sum(p * dw, axis=0, keepdims=True)) * 0.25
                ds = jnp.concatenate([pad, ds.astype(BF16)], axis=0)
                dq_ref[qk_rows(h), cols] = mm(ktx[qk_rows(h), keys], ds)
                dks.append(mm(qt_ref[qk_rows(h), cols], ds, NT))
                dvs.append(mm(dot_ref[v_rows(h), cols], wide, NT))
            for dst, rows, parts in ((dk_ref, qk_rows(h), dks), (dv_ref, v_rows(h), dvs)):
                dst[rows, 0:128] = parts[0][:, :128]
                dst[rows, 128:256] = parts[0][:, 128:] + parts[1][:, :128]
                dst[rows, 256:384] = parts[1][:, 128:]


def stage_mix(prefix_ref, qt_ref, dot_ref, num_ref, win_ref, gain_ref, dnum_ref, state_ref, outt):
    for group in range(HC // 4):
        states = []
        for i in range(4):
            h = group * 4 + i
            phi = features(qt_ref[qk_rows(h), :].astype(F32))
            main, rest = get_state(prefix_ref, group, i)
            num = num_ref[v_rows(h), :] + mm(main, phi[:128]) + mm(rest, phi[128:])
            inv = lax.rsqrt(jnp.mean(num * num, axis=0, keepdims=True) + EPS)
            gain = jnp.concatenate([gain_ref[v_rows(h), :]] * 2, axis=1)
            unit = num * inv
            outt[v_rows(h), :] = (unit * gain + win_ref[v_rows(h), :]).astype(BF16)
            dg = dot_ref[v_rows(h), :].astype(F32) * gain
            dnum = inv * (dg - unit * jnp.mean(dg * unit, axis=0, keepdims=True))
            half = dnum.astype(BF16)
            dnum_ref[v_rows(h), :] = half
            states.append(mm(half, phi, NT))
        put_state(state_ref, group, states)


def stage_back(prefix_ref, qt_ref, kt_ref, k_ref, v_ref, dnum_ref, dq_in, dk_ref, dv_ref, dqt):
    below = kernel_mask()

    @pl.loop(0, HC // 4)
    def _(group):
        for i in range(4):
            h = group * 4 + i
            pcol = pl.ds(pl.multiple_of((group * 2 + i // 2) * LANES, LANES), LANES)
            dk = dk_ref[qk_rows(h), :]
            dv = dv_ref[v_rows(h), :]
            main = prefix_ref[v_rows(h), :]
            rest = prefix_ref[pl.ds(pl.multiple_of(VW + group * 64, 64), 64), :][:, i * 32 : (i + 1) * 32]
            dnum = dnum_ref[v_rows(h), :]
            dphi = jnp.concatenate([mm(main, dnum, TN), mm(rest, dnum, TN)], axis=0)
            dq = dq_in[qk_rows(h), :] + features_back(dphi, qt_ref[qk_rows(h), :].astype(F32))
            dqs = []
            for j in range(2):
                cols = slice(j * 128, (j + 1) * 128)
                n = (j + 1) * 128
                s = tile_scores(k_ref[:n, :], qt_ref[:, cols], h)
                dn_pair = dnum_ref[pcol, cols]
                dn_one = jnp.where(head_mask(LANES, DV, i % 2), dn_pair, jnp.zeros_like(dn_pair))
                dkern = mm(v_ref[:n, pcol], dn_one)
                kern = 1.0 + s + 0.5 * s * s
                ds = dkern * (0.25 + 0.25 * s)
                if j == 0:
                    kern = jnp.where(below, kern, 0.0).astype(BF16)
                    ds = jnp.where(below, ds, 0.0).astype(BF16)
                else:
                    kern = jnp.concatenate(
                        [kern[:128].astype(BF16), jnp.where(below, kern[128:], 0.0).astype(BF16)], axis=0)
                    ds = jnp.concatenate(
                        [ds[:128].astype(BF16), jnp.where(below, ds[128:], 0.0).astype(BF16)], axis=0)
                dqs.append(mm(kt_ref[qk_rows(h), :n], ds))
                dka = mm(qt_ref[qk_rows(h), cols], ds, NT)
                dva = mm(dnum_ref[v_rows(h), cols], kern, NT)
                if j == 0:
                    dka = jnp.concatenate([dka, jnp.zeros_like(dka)], axis=1)
                    dva = jnp.concatenate([dva, jnp.zeros_like(dva)], axis=1)
                dk = dk + dka
                dv = dv + dva
            dqt[qk_rows(h), :] = dq + jnp.concatenate(dqs, axis=1)
            dk_ref[qk_rows(h), :] = dk
            dv_ref[v_rows(h), :] = dv


def stage_last(suffix_ref, kt_ref, vt_ref, dk_in, dv_in, dkt, dvt):
    for group in range(HC // 4):
        for i in range(4):
            h = group * 4 + i
            main, rest = get_state(suffix_ref, group, i)
            x = kt_ref[qk_rows(h), :].astype(F32)
            phi = features(x)
            vt = vt_ref[v_rows(h), :]
            dv = dv_in[v_rows(h), :] + mm(main, phi[:128]) + mm(rest, phi[128:])
            dphi = jnp.concatenate([mm(main, vt, TN), mm(rest, vt, TN)], axis=0)
            dk = dk_in[qk_rows(h), :] + features_back(dphi, x)
            dkt[qk_rows(h), :] = dk.astype(BF16)
            dvt[v_rows(h), :] = dv.astype(BF16)


def whole(n, rows, q_ref, k_ref, v_ref, do_ref, gain_in, out_ref, qg_ref, dkt, dvt,
          kt_o, vt_o, st_out, st2, sum1, got1, send2, base1, near1, prefix,
          dst2, sum3, got3, send4, base3, near3, suffix, rim_out, rim_in,
          qx, dox, qt, dot, dnum, outt, num, win, dq, dk, dv, dqt, kx, vx, ktx, vtx, gain,
          out_o, qg_o, dk_o, dv_o,
          send_sem, recv_sem, near_send, near_recv, pair_send, pair_recv, rim_send, rim_recv):
    me = lax.axis_index("seq")
    chips = n // 2
    planes = chips // 2
    chip = me // 2
    core = lax.rem(me, 2)
    far = 1 - core
    other = chip * 2 + far
    odd = lax.rem(chip, 2)
    barrier = pltpu.get_barrier_semaphore()

    @pl.loop(1, n)
    def _(step):
        pl.semaphore_signal(barrier, inc=1, device_id={"seq": lax.rem(me + step, n)},
                            device_id_type=pl.DeviceIdType.MESH)

    def remote(src, dst, ssem, rsem, to):
        return pltpu.make_async_remote_copy(
            src_ref=src, dst_ref=dst, send_sem=ssem, recv_sem=rsem,
            device_id={"seq": to}, device_id_type=pl.DeviceIdType.MESH)

    def chunk(ref, i):
        return ref.at[pl.ds(pl.multiple_of(i * rows, 16), rows), :]

    def cut(which, width):
        return pl.ds(pl.multiple_of(which * width, LANES), width)

    def pair_copy(index, src, dst):
        return remote(src, dst, pair_send.at[index], pair_recv.at[index], other)

    def is_in(span):
        return (chip >= span[0]) & (chip < span[1])

    def over(span, reach, body):
        lo, hi = span

        @pl.loop(lo, hi)
        def _(step):
            j = jnp.where(chip >= planes, step, lo + hi - 1 - step)

            @pl.when(j != chip)
            def _():
                body(j)

    def gather_copy(phase, src, dst, j):
        return remote(chunk(src, j), chunk(dst, chip), send_sem.at[phase, j], recv_sem.at[phase, chip], j * 2 + core)

    def gather_start(phase, span, src, dst):
        @pl.when(is_in(span))
        def _():
            over((0, chips), None, lambda j: gather_copy(phase, src, dst, j).start())

        chunk(dst, chip)[...] = chunk(src, chip)[...]

    def gather_wait(phase, span, src, dst):
        over(span, None, lambda j: remote(
            chunk(src, j), chunk(dst, j), send_sem.at[phase, j], recv_sem.at[phase, j], j * 2 + core).wait_recv())

        @pl.when(is_in(span))
        def _():
            over((0, chips), None, lambda j: gather_copy(phase, src, dst, j).wait_send())

    def spread_copy(phase, src, dst, j):
        return remote(chunk(src, j // 2), chunk(dst, chip), send_sem.at[phase, j], recv_sem.at[phase, chip],
                      j * 2 + core)

    def spread_start(phase, span, src, dst):
        over(span, None, lambda j: spread_copy(phase, src, dst, j).start())

        @pl.when(is_in(span))
        def _():
            chunk(dst, chip)[...] = chunk(src, chip // 2)[...]

        @pl.when(jnp.logical_not(is_in(span)))
        def _():
            dst[...] = jnp.zeros_like(dst)

    def spread_wait(phase, span, src, dst):
        @pl.when(is_in(span))
        def _():
            over((0, chips), None, lambda j: remote(
                chunk(src, j // 2), chunk(dst, j), send_sem.at[phase, j], recv_sem.at[phase, j],
                j * 2 + core).wait_recv())

        over(span, None, lambda j: spread_copy(phase, src, dst, j).wait_send())

    def near_copy(index, src, dst, to):
        return remote(src.at[0:PACKED, :], dst, near_send.at[index], near_recv.at[index], to * 2 + core)

    def scan(src, dst, reverse):
        def step(i, total):
            p = planes - 1 - i if reverse else i
            chunk(dst, p)[...] = total.astype(BF16)
            return total + (chunk(src, 2 * p)[...].astype(F32) + chunk(src, 2 * p + 1)[...].astype(F32))

        total = lax.fori_loop(0, planes - 1, step, jnp.zeros((rows, LANES), F32))
        chunk(dst, 0 if reverse else planes - 1)[...] = total.astype(BF16)

    def chip_sum(src, dst):
        dst[0:PACKED, :] = (src[0].astype(F32) + src[1].astype(F32)).astype(BF16)
        if chips * rows > PACKED:
            dst[PACKED:, :] = jnp.zeros((chips * rows - PACKED, LANES), BF16)

    early, late = (0, chips - 2), (2, chips)
    first_chip = chip == 0
    end_chip = chip == chips - 1
    after = jnp.minimum(chip + 1, chips - 1)
    before = jnp.maximum(chip - 1, 0)

    kt_own = ktx.at[core, :, 128:384]
    vt_own = vtx.at[core, :, 128:384]
    turn(kt_o, k_ref.at[:, cut(far, QW)])
    turn(vt_o, v_ref.at[:, cut(far, VW)])
    stage_state(kt_o, vt_o, st_out)
    pl.semaphore_wait(barrier, n - 1)

    state_copy = pair_copy(0, st_out, st2.at[core])
    state_copy.start()
    turn(kt_own, k_ref.at[:, cut(core, QW)])
    turn(vt_own, v_ref.at[:, cut(core, VW)])
    stage_state(kt_own, vt_own, st2.at[core])

    token_copies = [
        pair_copy(1, k_ref.at[:, cut(far, QW)], kx.at[core, 128:384, :]),
        pair_copy(2, v_ref.at[:, cut(far, VW)], vx.at[core, 128:384, :]),
        pair_copy(3, q_ref.at[:, cut(far, QW)], qx),
        pair_copy(4, do_ref.at[:, cut(far, VW)], dox),
    ]
    pair_copy(0, st_out, st2.at[far]).wait_recv()
    chip_sum(st2, sum1)
    gather_start(0, early, sum1, got1)

    @pl.when(odd == 0)
    def _():
        near_copy(0, sum1, near1, chip + 1).start()

    def rim_copies():
        tail = slice(BLK - WIN, BLK)
        return [remote(src.at[tail, c * w : (c + 1) * w], dst.at[0, 64:128, :], rim_send.at[2 * m + c],
                       rim_recv.at[m], after * 2 + c)
                for c in range(2) for m, (src, dst, w) in enumerate(((k_ref, kx, QW), (v_ref, vx, VW)))]

    sends_rim = (core == 1) & jnp.logical_not(end_chip)

    @pl.when(sends_rim)
    def _():
        for copy in rim_copies():
            copy.start()

    for copy in token_copies:
        copy.start()
    state_copy.wait_send()

    kx[core, 128:384, :] = k_ref[:, cut(core, QW)]
    vx[core, 128:384, :] = v_ref[:, cut(core, VW)]
    kx[0, 0:64, :] = jnp.zeros((64, QW), BF16)
    vx[0, 0:64, :] = jnp.zeros((64, VW), BF16)
    turn(qt.at[core], q_ref.at[:, cut(core, QW)])
    turn(dot.at[core], do_ref.at[:, cut(core, VW)])
    for c in range(VW // LANES):
        row = gain_in[pl.ds(core * (VW // LANES) + c, 1), :]
        gain[c * LANES : (c + 1) * LANES, :] = jnp.broadcast_to(row, (LANES, LANES)).T

    @pl.when(first_chip)
    def _():
        kx[0, 64:128, :] = jnp.zeros((64, QW), BF16)
        vx[0, 64:128, :] = jnp.zeros((64, VW), BF16)

    for copy in token_copies:
        copy.wait_send()
    arrivals = [
        pair_copy(1, k_ref.at[:, cut(far, QW)], kx.at[far, 128:384, :]),
        pair_copy(2, v_ref.at[:, cut(far, VW)], vx.at[far, 128:384, :]),
        token_copies[2], token_copies[3],
    ]
    for copy in arrivals:
        copy.wait_recv()
    turn(ktx.at[far, :, 128:384], kx.at[far, 128:384, :])
    turn(vtx.at[far, :, 128:384], vx.at[far, 128:384, :])
    turn(qt.at[far], qx)
    turn(dot.at[far], dox)
    kx[1, 0:128, :] = kx[0, 256:384, :]
    vx[1, 0:128, :] = vx[0, 256:384, :]
    ktx[1, :, 0:128] = ktx[0, :, 256:384]
    vtx[1, :, 0:128] = vtx[0, :, 256:384]

    def local(b):
        stage_local(first_chip if b == 0 else None, *(r.at[b] for r in (
            qt, dot, num, win, dq, dk, dv, kx, vx, ktx, vtx)))

    local(1)
    gather_wait(0, early, sum1, got1)
    scan(got1, send2, False)
    spread_start(1, late, send2, base1)

    @pl.when(jnp.logical_not(first_chip))
    def _():
        tail = slice(BLK - WIN, BLK)
        for m, (src, dst, w) in enumerate(((k_ref, kx, QW), (v_ref, vx, VW))):
            remote(src.at[tail, 0:w], dst.at[0, 64:128, :], rim_send.at[2 * m], rim_recv.at[m], me).wait_recv()

    @pl.when(sends_rim)
    def _():
        for copy in rim_copies():
            copy.wait_send()

    turn(ktx.at[0, :, 0:128], kx.at[0, 0:128, :])
    turn(vtx.at[0, :, 0:128], vx.at[0, 0:128, :])
    local(0)

    for ref, at, lo in ((dk, 0, 0), (dv, QW, QW)):
        size = ref.shape[1] // 2
        top = ref[0, 0:size, 0:128]
        rim_out[lo // 2 : lo // 2 + size, :] = (pltpu.roll(top, 64, 1) + ref[0, size : 2 * size, 0:128]).astype(BF16)

    @pl.when(odd == 1)
    def _():
        near_copy(0, sum1, near1, chip).wait_recv()

    @pl.when(odd == 0)
    def _():
        near_copy(0, sum1, near1, chip + 1).wait_send()
        near1[...] = jnp.zeros_like(near1)

    spread_wait(1, late, send2, base1)

    def rim_back(to):
        return remote(rim_out, rim_in, rim_send.at[4], rim_recv.at[2], to * 2 + core)

    @pl.when(jnp.logical_not(first_chip))
    def _():
        rim_back(before).start()

    def bases(base, near, state, dst, order):
        total = base[0:PACKED, :].astype(F32) + near[...].astype(F32)
        dst[order[0]] = total.astype(BF16)
        dst[order[1]] = (total + state[order[0]].astype(F32)).astype(BF16)

    bases(base1, near1, st2, prefix, (0, 1))
    for b in range(2):
        stage_mix(*(r.at[b] for r in (prefix, qt, dot, num, win)), gain, dnum.at[b], dst2.at[b], outt.at[b])

    chip_sum(dst2, sum3)
    gather_start(2, late, sum3, got3)

    @pl.when(odd == 1)
    def _():
        near_copy(1, sum3, near3, chip - 1).start()

    turn_out(out_o, outt.at[far])
    out_copy = pair_copy(5, out_o, out_ref.at[:, cut(core, VW)])
    out_copy.start()
    turn_out(out_ref.at[:, cut(core, VW)], outt.at[core])

    def back(b):
        stage_back(*(r.at[b] for r in (prefix, qt)), ktx.at[b, :, 128:384], kx.at[b, 128:384, :],
                   vx.at[b, 128:384, :], dnum.at[b], dq.at[b], dk.at[b, :, 128:384], dv.at[b, :, 128:384], dqt.at[b])

    back(0)
    gather_wait(2, late, sum3, got3)
    scan(got3, send4, True)
    spread_start(3, early, send4, base3)
    back(1)
    turn_out(qg_o, dqt.at[far])
    qg_copy = pair_copy(6, qg_o, qg_ref.at[:, cut(core, QW)])
    qg_copy.start()
    turn_out(qg_ref.at[:, cut(core, QW)], dqt.at[core])

    @pl.when(end_chip)
    def _():
        rim_in[...] = jnp.zeros_like(rim_in)

    @pl.when(jnp.logical_not(end_chip))
    def _():
        rim_back(after).wait_recv()

    @pl.when(jnp.logical_not(first_chip))
    def _():
        rim_back(before).wait_send()

    for ref, lo in ((dk, 0), (dv, QW)):
        size = ref.shape[1] // 2
        ref[0, :, 256:384] = ref[0, :, 256:384] + ref[1, :, 0:128]
        got = rim_in[lo // 2 : lo // 2 + size, :].astype(F32)
        upper = lax.broadcasted_iota(jnp.int32, got.shape, 1) >= 64
        zero = jnp.zeros_like(got)
        ref[1, 0:size, 256:384] = ref[1, 0:size, 256:384] + jnp.where(upper, pltpu.roll(got, 64, 1), zero)
        ref[1, size : 2 * size, 256:384] = ref[1, size : 2 * size, 256:384] + jnp.where(upper, got, zero)

    @pl.when(odd == 0)
    def _():
        near_copy(1, sum3, near3, chip).wait_recv()

    @pl.when(odd == 1)
    def _():
        near_copy(1, sum3, near3, chip - 1).wait_send()
        near3[...] = jnp.zeros_like(near3)

    spread_wait(3, early, send4, base3)
    bases(base3, near3, dst2, suffix, (1, 0))

    def last(b, dk_to, dv_to):
        stage_last(suffix.at[b], ktx.at[b, :, 128:384], vtx.at[b, :, 128:384],
                   dk.at[b, :, 128:384], dv.at[b, :, 128:384], dk_to, dv_to)

    dk_rows = pl.ds(pl.multiple_of(core * QW, QW), QW)
    dv_rows = pl.ds(pl.multiple_of(core * VW, VW), VW)
    last(far, dk_o, dv_o)
    ends = [pair_copy(7, dk_o, dkt.at[dk_rows, :]), pair_copy(8, dv_o, dvt.at[dv_rows, :])]
    for copy in ends:
        copy.start()
    last(core, dkt.at[dk_rows, :], dvt.at[dv_rows, :])
    dk_back = pl.ds(pl.multiple_of(far * QW, QW), QW)
    dv_back = pl.ds(pl.multiple_of(far * VW, VW), VW)
    returns = [
        pair_copy(5, out_o, out_ref.at[:, cut(far, VW)]), pair_copy(6, qg_o, qg_ref.at[:, cut(far, QW)]),
        pair_copy(7, dk_o, dkt.at[dk_back, :]), pair_copy(8, dv_o, dvt.at[dv_back, :]),
    ]
    for copy in returns:
        copy.wait_recv()
        copy.wait_send()


def turn_out(dst, src):
    for c in range(dst.shape[1] // LANES):
        cols = slice(c * LANES, (c + 1) * LANES)
        dst[:, cols] = src[cols, :].T.astype(BF16)


def finish(out_in, qg_in, dkt, dvt, out_ref, qg_ref, kg_ref, vg_ref):
    out_ref[...] = out_in[...]
    qg_ref[...] = qg_in[...]
    turn_out(kg_ref, dkt)
    turn_out(vg_ref, dvt)


def on_device(q, k, v, do, gain):
    n = lax.axis_size("seq")
    chips = n // 2
    rows = -(-PACKED // (16 * chips)) * 16
    vm = pltpu.VMEM

    def both(*shape, dtype=BF16):
        return vm((2,) + shape, dtype)

    packed = vm((PACKED, LANES), BF16)
    ring = vm((chips * rows, LANES), BF16)
    small = vm((chips // 2 * rows, LANES), BF16)
    rim = vm(((QW + VW) // 2, LANES), BF16)
    outs = pl.pallas_call(
        functools.partial(whole, n, rows),
        out_shape=[jax.ShapeDtypeStruct(x.shape, BF16) for x in (do, q)] + [
            jax.ShapeDtypeStruct(s, BF16) for s in ((H * FD, BLK), (H * DV, BLK))],
        in_specs=[pl.BlockSpec(memory_space=vm)] * 5,
        out_specs=[pl.BlockSpec(memory_space=vm)] * 4,
        scratch_shapes=[
            vm((QW, BLK), BF16), vm((VW, BLK), BF16), packed,
            both(PACKED, LANES), ring, ring, small, ring, packed, both(PACKED, LANES),
            both(PACKED, LANES), ring, ring, small, ring, packed, both(PACKED, LANES),
            rim, rim, vm((BLK, QW), BF16), vm((BLK, VW), BF16),
            both(QW, BLK), both(VW, BLK), both(VW, BLK), both(VW, BLK),
            both(VW, BLK, dtype=F32), both(VW, BLK, dtype=F32), both(QW, BLK, dtype=F32),
            both(QW, 384, dtype=F32), both(VW, 384, dtype=F32), both(QW, BLK, dtype=F32),
            both(384, QW), both(384, VW), both(QW, 384), both(VW, 384),
            vm((VW, LANES), F32),
            vm((BLK, VW), BF16), vm((BLK, QW), BF16), vm((QW, BLK), BF16), vm((VW, BLK), BF16),
            pltpu.SemaphoreType.DMA((4, chips)), pltpu.SemaphoreType.DMA((4, chips)),
            pltpu.SemaphoreType.DMA((2,)), pltpu.SemaphoreType.DMA((2,)),
            pltpu.SemaphoreType.DMA((9,)), pltpu.SemaphoreType.DMA((9,)),
            pltpu.SemaphoreType.DMA((5,)), pltpu.SemaphoreType.DMA((3,)),
        ],
        compiler_params=pltpu.CompilerParams(
            vmem_limit_bytes=56 * 1024 * 1024, collective_id=0, has_side_effects=True),
    )(q, k, v, do, gain.reshape(H * DV // LANES, LANES))
    steps = 2
    whole_cols = [pl.BlockSpec((BLK, x // steps), lambda i: (0, i)) for x in (H * DV, H * FD, H * FD, H * DV)]
    turned = [pl.BlockSpec((x // steps, BLK), lambda i: (i, 0)) for x in (H * FD, H * DV)]
    return pl.pallas_call(
        finish,
        grid=(steps,),
        out_shape=[jax.ShapeDtypeStruct(x.shape, BF16) for x in (do, q, k, v)],
        in_specs=whole_cols[:2] + turned,
        out_specs=whole_cols,
    )(*outs)


def solution(mesh):
    split = P(("groups", "seq"), None)
    return jax.shard_map(
        on_device, mesh=mesh, in_specs=(split,) * 4 + (P(),), out_specs=(split,) * 4, check_vma=False
    )
```

```python
import functools

import jax
import jax.numpy as jnp
from jax import lax
from jax.experimental import pallas as pl
from jax.experimental.pallas import tpu as pltpu
from jax.sharding import PartitionSpec as P

H = 16
FD = 16
DV = 64
WIN = 64
BLK = 256
LANES = 128
HC = H // 2
QW = HC * FD
VW = HC * DV
PACKED = VW + VW // 4
QUAD = 0.17677669529663687
EPS = 1e-06
NEG = -1e30
SPANS = ((0, H * DV), (H * DV, H * (DV + FD)), (H * (DV + FD), H * (DV + 2 * FD)), (H * (DV + 2 * FD), H * 2 * (DV + FD)))
F32 = jnp.float32
BF16 = jnp.bfloat16

NN = (((1,), (0,)), ((), ()))
NT = (((1,), (1,)), ((), ()))
TN = (((0,), (0,)), ((), ()))


def mm(a, b, dims=NN):
    return lax.dot_general(a, b, dims, preferred_element_type=F32)


def features(x):
    parts = [x * x * QUAD]
    for d in range(1, 8):
        parts.append(x * pltpu.roll(x, FD - d, 0) * 0.25)
    parts.append(x[:8] * x[8:] * 0.25)
    row = lax.broadcasted_iota(jnp.int32, (8, x.shape[1]), 0)
    parts.append(jnp.where(row == 0, 1.0, 0.0).astype(F32))
    parts.append(x * 0.5)
    return jnp.concatenate(parts, axis=0).astype(BF16)


def features_back(g, x):
    dx = (2.0 * QUAD) * g[:FD] * x
    for d in range(1, 8):
        part = g[d * FD : (d + 1) * FD] * 0.25
        dx = dx + part * pltpu.roll(x, FD - d, 0) + pltpu.roll(part * x, d, 0)
    half = g[128:136] * 0.25
    dx = dx + jnp.concatenate([half * x[8:], half * x[:8]], axis=0)
    return dx + 0.5 * g[144:160]


def turn(dst, src):
    for c in range(src.shape[1] // LANES):
        cols = slice(c * LANES, (c + 1) * LANES)
        dst[cols, :] = src[:, cols].T


def put_state(buf, group, states):
    for i, st in enumerate(states):
        at = group * 256 + i * 64
        buf[at : at + 64, :] = st[:, :128].astype(BF16)
    rest = jnp.concatenate([st[:, 128:160] for st in states], axis=1)
    buf[VW + group * 64 : VW + group * 64 + 64, :] = rest.astype(BF16)


def get_state(buf, group, i):
    at = group * 256 + i * 64
    main = buf[at : at + 64, :]
    rest = buf[VW + group * 64 : VW + group * 64 + 64, :][:, i * 32 : (i + 1) * 32]
    return main, rest


def qk_rows(h):
    return pl.ds(pl.multiple_of(h * FD, FD), FD) if not isinstance(h, int) else slice(h * FD, (h + 1) * FD)


def v_rows(h):
    return pl.ds(pl.multiple_of(h * DV, DV), DV) if not isinstance(h, int) else slice(h * DV, (h + 1) * DV)


def head_mask(rows, width, which):
    row = lax.broadcasted_iota(jnp.int32, (128, rows), 0)
    return (row >= which * width) & (row < (which + 1) * width)


def tile_scores(kx, q_all, head):
    zero = jnp.zeros_like(q_all)
    picked = jnp.where(head_mask(LANES, FD, head), q_all, zero)
    return mm(kx, picked) * 0.25


def kernel_mask():
    r = lax.broadcasted_iota(jnp.int32, (128, 128), 0)
    c = lax.broadcasted_iota(jnp.int32, (128, 128), 1)
    return r <= c


def stage_state(kt, vt, state):
    for group in range(HC // 4):
        states = []
        for i in range(4):
            h = group * 4 + i
            phi = features(kt[qk_rows(h), :].astype(F32))
            states.append(mm(vt[v_rows(h), :], phi, NT))
        put_state(state, group, states)


def stage_local(first, qt_ref, dot_ref, num_ref, win_ref, dq_ref, dk_ref, dv_ref, kx, vx, ktx, vtx):
    r = lax.broadcasted_iota(jnp.int32, (192, 128), 0)
    c = lax.broadcasted_iota(jnp.int32, (192, 128), 1)
    band = (r >= c + 1) & (r <= c + 64)
    band0 = band if first is None else band & (r >= jnp.where(first, 64, 0))
    below = kernel_mask()

    @pl.loop(0, HC // 2)
    def _(pair):
        prow = pl.ds(pl.multiple_of(pair * LANES, LANES), LANES)
        for i in range(2):
            h = pair * 2 + i
            dks = []
            dvs = []
            for j in range(2):
                cols = slice(j * 128, (j + 1) * 128)
                keys = slice(j * 128, j * 128 + 256)
                s = tile_scores(kx[keys, :], qt_ref[:, cols], h)
                kern = 1.0 + s + 0.5 * s * s
                last = jnp.where(below, kern[128:], 0.0).astype(BF16)
                if j == 0:
                    local = mm(vtx[v_rows(h), 128:256], last)
                else:
                    local = mm(vtx[v_rows(h), 128:384],
                               jnp.concatenate([kern[:128].astype(BF16), last], axis=0))
                num_ref[v_rows(h), cols] = local
                sw = jnp.where(band0 if j == 0 else band, s[64:], NEG)
                e = jnp.exp(sw - jnp.max(sw, axis=0, keepdims=True))
                p = e * (1.0 / jnp.sum(e, axis=0, keepdims=True))
                w = p.astype(BF16)
                pad = jnp.zeros((64, 128), BF16)
                wide = jnp.concatenate([pad, w], axis=0)
                win_ref[v_rows(h), cols] = mm(vtx[v_rows(h), keys], wide)
                do_pair = dot_ref[prow, cols]
                do_one = jnp.where(head_mask(LANES, DV, i), do_pair, jnp.zeros_like(do_pair))
                vpair = vx[j * 128 + 64 : j * 128 + 256, prow]
                dw = mm(vpair, do_one)
                ds = p * (dw - jnp.sum(p * dw, axis=0, keepdims=True)) * 0.25
                ds = jnp.concatenate([pad, ds.astype(BF16)], axis=0)
                dq_ref[qk_rows(h), cols] = mm(ktx[qk_rows(h), keys], ds)
                dks.append(mm(qt_ref[qk_rows(h), cols], ds, NT))
                dvs.append(mm(dot_ref[v_rows(h), cols], wide, NT))
            for dst, rows, parts in ((dk_ref, qk_rows(h), dks), (dv_ref, v_rows(h), dvs)):
                dst[rows, 0:128] = parts[0][:, :128]
                dst[rows, 128:256] = parts[0][:, 128:] + parts[1][:, :128]
                dst[rows, 256:384] = parts[1][:, 128:]


def stage_mix(prefix_ref, qt_ref, dot_ref, num_ref, win_ref, gain_ref, dnum_ref, state_ref, outt):
    for group in range(HC // 4):
        states = []
        for i in range(4):
            h = group * 4 + i
            phi = features(qt_ref[qk_rows(h), :].astype(F32))
            main, rest = get_state(prefix_ref, group, i)
            num = num_ref[v_rows(h), :] + mm(main, phi[:128]) + mm(rest, phi[128:])
            inv = lax.rsqrt(jnp.mean(num * num, axis=0, keepdims=True) + EPS)
            gain = jnp.concatenate([gain_ref[v_rows(h), :]] * 2, axis=1)
            unit = num * inv
            outt[v_rows(h), :] = (unit * gain + win_ref[v_rows(h), :]).astype(BF16)
            dg = dot_ref[v_rows(h), :].astype(F32) * gain
            dnum = inv * (dg - unit * jnp.mean(dg * unit, axis=0, keepdims=True))
            half = dnum.astype(BF16)
            dnum_ref[v_rows(h), :] = half
            states.append(mm(half, phi, NT))
        put_state(state_ref, group, states)


def stage_back(prefix_ref, qt_ref, kt_ref, k_ref, v_ref, dnum_ref, dq_in, dk_ref, dv_ref, dqt):
    below = kernel_mask()

    @pl.loop(0, HC // 4)
    def _(group):
        for i in range(4):
            h = group * 4 + i
            pcol = pl.ds(pl.multiple_of((group * 2 + i // 2) * LANES, LANES), LANES)
            dk = dk_ref[qk_rows(h), :]
            dv = dv_ref[v_rows(h), :]
            main = prefix_ref[v_rows(h), :]
            rest = prefix_ref[pl.ds(pl.multiple_of(VW + group * 64, 64), 64), :][:, i * 32 : (i + 1) * 32]
            dnum = dnum_ref[v_rows(h), :]
            dphi = jnp.concatenate([mm(main, dnum, TN), mm(rest, dnum, TN)], axis=0)
            dq = dq_in[qk_rows(h), :] + features_back(dphi, qt_ref[qk_rows(h), :].astype(F32))
            dqs = []
            for j in range(2):
                cols = slice(j * 128, (j + 1) * 128)
                n = (j + 1) * 128
                s = tile_scores(k_ref[:n, :], qt_ref[:, cols], h)
                dn_pair = dnum_ref[pcol, cols]
                dn_one = jnp.where(head_mask(LANES, DV, i % 2), dn_pair, jnp.zeros_like(dn_pair))
                dkern = mm(v_ref[:n, pcol], dn_one)
                kern = 1.0 + s + 0.5 * s * s
                ds = dkern * (0.25 + 0.25 * s)
                if j == 0:
                    kern = jnp.where(below, kern, 0.0).astype(BF16)
                    ds = jnp.where(below, ds, 0.0).astype(BF16)
                else:
                    kern = jnp.concatenate(
                        [kern[:128].astype(BF16), jnp.where(below, kern[128:], 0.0).astype(BF16)], axis=0)
                    ds = jnp.concatenate(
                        [ds[:128].astype(BF16), jnp.where(below, ds[128:], 0.0).astype(BF16)], axis=0)
                dqs.append(mm(kt_ref[qk_rows(h), :n], ds))
                dka = mm(qt_ref[qk_rows(h), cols], ds, NT)
                dva = mm(dnum_ref[v_rows(h), cols], kern, NT)
                if j == 0:
                    dka = jnp.concatenate([dka, jnp.zeros_like(dka)], axis=1)
                    dva = jnp.concatenate([dva, jnp.zeros_like(dva)], axis=1)
                dk = dk + dka
                dv = dv + dva
            dqt[qk_rows(h), :] = dq + jnp.concatenate(dqs, axis=1)
            dk_ref[qk_rows(h), :] = dk
            dv_ref[v_rows(h), :] = dv


def stage_last(suffix_ref, kt_ref, vt_ref, dk_in, dv_in, dkt, dvt):
    for group in range(HC // 4):
        for i in range(4):
            h = group * 4 + i
            main, rest = get_state(suffix_ref, group, i)
            x = kt_ref[qk_rows(h), :].astype(F32)
            phi = features(x)
            vt = vt_ref[v_rows(h), :]
            dv = dv_in[v_rows(h), :] + mm(main, phi[:128]) + mm(rest, phi[128:])
            dphi = jnp.concatenate([mm(main, vt, TN), mm(rest, vt, TN)], axis=0)
            dk = dk_in[qk_rows(h), :] + features_back(dphi, x)
            dkt[qk_rows(h), :] = dk.astype(BF16)
            dvt[v_rows(h), :] = dv.astype(BF16)


def whole(n, rows, q_hbm, k_hbm, v_hbm, do_hbm, gain_hbm, res,
          k_far, v_far, q_far, do_far, q_own, do_own, gain_in, load_sem,
          kt_o, vt_o, st_out, st2, sum1, got1, send2, base1, near1, prefix,
          dst2, sum3, got3, send4, base3, near3, suffix, rim_out, rim_in,
          qx, dox, qt, dot, dnum, outt, num, win, dq, dk, dv, dqt, kx, vx, ktx, vtx, gain,
          out_o, qg_o, kg_o, vg_o, dkt, dvt,
          send_sem, recv_sem, near_send, near_recv, pair_send, pair_recv, rim_send, rim_recv):
    me = lax.axis_index("seq")
    out_ref, qg_ref, kg_ref, vg_ref = (res.at[:, a:b] for a, b in SPANS)
    chips = n // 2
    planes = chips // 2
    chip = me // 2
    core = lax.rem(me, 2)
    far = 1 - core
    other = chip * 2 + far
    odd = lax.rem(chip, 2)
    barrier = pltpu.get_barrier_semaphore()

    @pl.loop(1, n)
    def _(step):
        pl.semaphore_signal(barrier, inc=1, device_id={"seq": lax.rem(me + step, n)},
                            device_id_type=pl.DeviceIdType.MESH)

    def load(index, src, dst):
        copy = pltpu.make_async_copy(src, dst, load_sem.at[index])
        copy.start()
        return copy

    def columns(which, width):
        return pl.ds(pl.multiple_of(which * width, LANES), width)

    loads = [load(i, src.at[:, columns(which, w)], dst) for i, (src, which, w, dst) in enumerate((
        (k_hbm, far, QW, k_far), (v_hbm, far, VW, v_far),
        (k_hbm, core, QW, kx.at[core, 128:384, :]), (v_hbm, core, VW, vx.at[core, 128:384, :]),
        (q_hbm, far, QW, q_far), (do_hbm, far, VW, do_far),
        (q_hbm, core, QW, q_own), (do_hbm, core, VW, do_own)))]
    loads.append(load(8, gain_hbm, gain_in))

    def remote(src, dst, ssem, rsem, to):
        return pltpu.make_async_remote_copy(
            src_ref=src, dst_ref=dst, send_sem=ssem, recv_sem=rsem,
            device_id={"seq": to}, device_id_type=pl.DeviceIdType.MESH)

    def chunk(ref, i):
        return ref.at[pl.ds(pl.multiple_of(i * rows, 16), rows), :]

    def cut(which, width):
        return pl.ds(pl.multiple_of(which * width, LANES), width)

    def pair_copy(index, src, dst):
        return remote(src, dst, pair_send.at[index], pair_recv.at[index], other)

    def is_in(span):
        return (chip >= span[0]) & (chip < span[1])

    def over(span, reach, body):
        lo, hi = span

        @pl.loop(lo, hi)
        def _(step):
            j = jnp.where(chip >= planes, step, lo + hi - 1 - step)

            @pl.when(j != chip)
            def _():
                body(j)

    def gather_copy(phase, src, dst, j):
        return remote(chunk(src, j), chunk(dst, chip), send_sem.at[phase, j], recv_sem.at[phase, chip], j * 2 + core)

    def gather_start(phase, span, src, dst):
        @pl.when(is_in(span))
        def _():
            over((0, chips), None, lambda j: gather_copy(phase, src, dst, j).start())

        chunk(dst, chip)[...] = chunk(src, chip)[...]

    def gather_wait(phase, span, src, dst):
        over(span, None, lambda j: remote(
            chunk(src, j), chunk(dst, j), send_sem.at[phase, j], recv_sem.at[phase, j], j * 2 + core).wait_recv())

        @pl.when(is_in(span))
        def _():
            over((0, chips), None, lambda j: gather_copy(phase, src, dst, j).wait_send())

    def spread_copy(phase, src, dst, j):
        return remote(chunk(src, j // 2), chunk(dst, chip), send_sem.at[phase, j], recv_sem.at[phase, chip],
                      j * 2 + core)

    def spread_start(phase, span, src, dst):
        over(span, None, lambda j: spread_copy(phase, src, dst, j).start())

        @pl.when(is_in(span))
        def _():
            chunk(dst, chip)[...] = chunk(src, chip // 2)[...]

        @pl.when(jnp.logical_not(is_in(span)))
        def _():
            dst[...] = jnp.zeros_like(dst)

    def spread_wait(phase, span, src, dst):
        @pl.when(is_in(span))
        def _():
            over((0, chips), None, lambda j: remote(
                chunk(src, j // 2), chunk(dst, j), send_sem.at[phase, j], recv_sem.at[phase, j],
                j * 2 + core).wait_recv())

        over(span, None, lambda j: spread_copy(phase, src, dst, j).wait_send())

    def near_copy(index, src, dst, to):
        return remote(src.at[0:PACKED, :], dst, near_send.at[index], near_recv.at[index], to * 2 + core)

    def scan(src, dst, reverse):
        def step(i, total):
            p = planes - 1 - i if reverse else i
            chunk(dst, p)[...] = total.astype(BF16)
            return total + (chunk(src, 2 * p)[...].astype(F32) + chunk(src, 2 * p + 1)[...].astype(F32))

        total = lax.fori_loop(0, planes - 1, step, jnp.zeros((rows, LANES), F32))
        chunk(dst, 0 if reverse else planes - 1)[...] = total.astype(BF16)

    def chip_sum(src, dst):
        dst[0:PACKED, :] = (src[0].astype(F32) + src[1].astype(F32)).astype(BF16)
        if chips * rows > PACKED:
            dst[PACKED:, :] = jnp.zeros((chips * rows - PACKED, LANES), BF16)

    early, late = (0, chips - 2), (2, chips)
    first_chip = chip == 0
    end_chip = chip == chips - 1
    after = jnp.minimum(chip + 1, chips - 1)
    before = jnp.maximum(chip - 1, 0)

    kt_own = ktx.at[core, :, 128:384]
    vt_own = vtx.at[core, :, 128:384]
    loads[0].wait()
    turn(kt_o, k_far)
    loads[1].wait()
    turn(vt_o, v_far)
    stage_state(kt_o, vt_o, st_out)
    pl.semaphore_wait(barrier, n - 1)

    state_copy = pair_copy(0, st_out, st2.at[core])
    state_copy.start()
    loads[2].wait()
    turn(kt_own, kx.at[core, 128:384, :])
    loads[3].wait()
    turn(vt_own, vx.at[core, 128:384, :])
    stage_state(kt_own, vt_own, st2.at[core])

    token_copies = [
        pair_copy(1, k_far, kx.at[core, 128:384, :]),
        pair_copy(2, v_far, vx.at[core, 128:384, :]),
        pair_copy(3, q_far, qx),
        pair_copy(4, do_far, dox),
    ]
    pair_copy(0, st_out, st2.at[far]).wait_recv()
    chip_sum(st2, sum1)
    gather_start(0, early, sum1, got1)

    @pl.when(odd == 0)
    def _():
        near_copy(0, sum1, near1, chip + 1).start()

    def rim_copies():
        tail = slice(BLK - WIN, BLK)
        return [remote(src, dst.at[0, 64:128, :], rim_send.at[2 * m + c], rim_recv.at[m], after * 2 + c)
                for m, (dst, own_src, far_src) in enumerate(((kx, kx, k_far), (vx, vx, v_far)))
                for c, src in enumerate((far_src.at[tail, :], own_src.at[1, 320:384, :]))]

    sends_rim = (core == 1) & jnp.logical_not(end_chip)

    @pl.when(sends_rim)
    def _():
        for copy in rim_copies():
            copy.start()

    loads[4].wait()
    loads[5].wait()
    for copy in token_copies:
        copy.start()
    state_copy.wait_send()

    kx[0, 0:64, :] = jnp.zeros((64, QW), BF16)
    vx[0, 0:64, :] = jnp.zeros((64, VW), BF16)
    for copy in loads[6:]:
        copy.wait()
    turn(qt.at[core], q_own)
    turn(dot.at[core], do_own)
    for c in range(VW // LANES):
        row = gain_in[pl.ds(core * (VW // LANES) + c, 1), :]
        gain[c * LANES : (c + 1) * LANES, :] = jnp.broadcast_to(row, (LANES, LANES)).T

    @pl.when(first_chip)
    def _():
        kx[0, 64:128, :] = jnp.zeros((64, QW), BF16)
        vx[0, 64:128, :] = jnp.zeros((64, VW), BF16)

    for copy in token_copies:
        copy.wait_send()
    arrivals = [
        pair_copy(1, k_far, kx.at[far, 128:384, :]),
        pair_copy(2, v_far, vx.at[far, 128:384, :]),
        token_copies[2], token_copies[3],
    ]
    for copy in arrivals:
        copy.wait_recv()
    turn(ktx.at[far, :, 128:384], kx.at[far, 128:384, :])
    turn(vtx.at[far, :, 128:384], vx.at[far, 128:384, :])
    turn(qt.at[far], qx)
    turn(dot.at[far], dox)
    kx[1, 0:128, :] = kx[0, 256:384, :]
    vx[1, 0:128, :] = vx[0, 256:384, :]
    ktx[1, :, 0:128] = ktx[0, :, 256:384]
    vtx[1, :, 0:128] = vtx[0, :, 256:384]

    def local(b):
        stage_local(first_chip if b == 0 else None, *(r.at[b] for r in (
            qt, dot, num, win, dq, dk, dv, kx, vx, ktx, vtx)))

    local(1)
    gather_wait(0, early, sum1, got1)
    scan(got1, send2, False)
    spread_start(1, late, send2, base1)

    @pl.when(jnp.logical_not(first_chip))
    def _():
        tail = slice(BLK - WIN, BLK)
        for m, (src, dst) in enumerate(((k_far, kx), (v_far, vx))):
            remote(src.at[tail, :], dst.at[0, 64:128, :], rim_send.at[2 * m], rim_recv.at[m], me).wait_recv()

    @pl.when(sends_rim)
    def _():
        for copy in rim_copies():
            copy.wait_send()

    turn(ktx.at[0, :, 0:128], kx.at[0, 0:128, :])
    turn(vtx.at[0, :, 0:128], vx.at[0, 0:128, :])
    local(0)

    for ref, at, lo in ((dk, 0, 0), (dv, QW, QW)):
        size = ref.shape[1] // 2
        top = ref[0, 0:size, 0:128]
        rim_out[lo // 2 : lo // 2 + size, :] = (pltpu.roll(top, 64, 1) + ref[0, size : 2 * size, 0:128]).astype(BF16)

    @pl.when(odd == 1)
    def _():
        near_copy(0, sum1, near1, chip).wait_recv()

    @pl.when(odd == 0)
    def _():
        near_copy(0, sum1, near1, chip + 1).wait_send()
        near1[...] = jnp.zeros_like(near1)

    spread_wait(1, late, send2, base1)

    def rim_back(to):
        return remote(rim_out, rim_in, rim_send.at[4], rim_recv.at[2], to * 2 + core)

    @pl.when(jnp.logical_not(first_chip))
    def _():
        rim_back(before).start()

    def bases(base, near, state, dst, order):
        total = base[0:PACKED, :].astype(F32) + near[...].astype(F32)
        dst[order[0]] = total.astype(BF16)
        dst[order[1]] = (total + state[order[0]].astype(F32)).astype(BF16)

    bases(base1, near1, st2, prefix, (0, 1))
    for b in range(2):
        stage_mix(*(r.at[b] for r in (prefix, qt, dot, num, win)), gain, dnum.at[b], dst2.at[b], outt.at[b])

    chip_sum(dst2, sum3)
    gather_start(2, late, sum3, got3)

    @pl.when(odd == 1)
    def _():
        near_copy(1, sum3, near3, chip - 1).start()

    turn_out(out_o, outt.at[far])
    out_copy = pair_copy(5, out_o, out_ref.at[:, cut(core, VW)])
    out_copy.start()
    turn_out(out_ref.at[:, cut(core, VW)], outt.at[core])

    def back(b):
        stage_back(*(r.at[b] for r in (prefix, qt)), ktx.at[b, :, 128:384], kx.at[b, 128:384, :],
                   vx.at[b, 128:384, :], dnum.at[b], dq.at[b], dk.at[b, :, 128:384], dv.at[b, :, 128:384], dqt.at[b])

    back(0)
    gather_wait(2, late, sum3, got3)
    scan(got3, send4, True)
    spread_start(3, early, send4, base3)
    back(1)
    turn_out(qg_o, dqt.at[far])
    qg_copy = pair_copy(6, qg_o, qg_ref.at[:, cut(core, QW)])
    qg_copy.start()
    turn_out(qg_ref.at[:, cut(core, QW)], dqt.at[core])

    @pl.when(end_chip)
    def _():
        rim_in[...] = jnp.zeros_like(rim_in)

    @pl.when(jnp.logical_not(end_chip))
    def _():
        rim_back(after).wait_recv()

    @pl.when(jnp.logical_not(first_chip))
    def _():
        rim_back(before).wait_send()

    for ref, lo in ((dk, 0), (dv, QW)):
        size = ref.shape[1] // 2
        ref[0, :, 256:384] = ref[0, :, 256:384] + ref[1, :, 0:128]
        got = rim_in[lo // 2 : lo // 2 + size, :].astype(F32)
        upper = lax.broadcasted_iota(jnp.int32, got.shape, 1) >= 64
        zero = jnp.zeros_like(got)
        ref[1, 0:size, 256:384] = ref[1, 0:size, 256:384] + jnp.where(upper, pltpu.roll(got, 64, 1), zero)
        ref[1, size : 2 * size, 256:384] = ref[1, size : 2 * size, 256:384] + jnp.where(upper, got, zero)

    @pl.when(odd == 0)
    def _():
        near_copy(1, sum3, near3, chip).wait_recv()

    @pl.when(odd == 1)
    def _():
        near_copy(1, sum3, near3, chip - 1).wait_send()
        near3[...] = jnp.zeros_like(near3)

    spread_wait(3, early, send4, base3)
    bases(base3, near3, dst2, suffix, (1, 0))

    def last(b, dk_to, dv_to):
        stage_last(suffix.at[b], ktx.at[b, :, 128:384], vtx.at[b, :, 128:384],
                   dk.at[b, :, 128:384], dv.at[b, :, 128:384], dk_to, dv_to)

    last(far, dkt.at[0], dvt.at[0])
    turn_out(kg_o, dkt.at[0])
    turn_out(vg_o, dvt.at[0])
    ends = [pair_copy(7, kg_o, kg_ref.at[:, cut(core, QW)]), pair_copy(8, vg_o, vg_ref.at[:, cut(core, VW)])]
    for copy in ends:
        copy.start()
    last(core, dkt.at[1], dvt.at[1])
    turn_out(kg_ref.at[:, cut(core, QW)], dkt.at[1])
    turn_out(vg_ref.at[:, cut(core, VW)], dvt.at[1])
    returns = [
        pair_copy(5, out_o, out_ref.at[:, cut(far, VW)]), pair_copy(6, qg_o, qg_ref.at[:, cut(far, QW)]),
        pair_copy(7, kg_o, kg_ref.at[:, cut(far, QW)]), pair_copy(8, vg_o, vg_ref.at[:, cut(far, VW)]),
    ]
    for copy in returns:
        copy.wait_recv()
        copy.wait_send()


def turn_out(dst, src):
    for c in range(dst.shape[1] // LANES):
        cols = slice(c * LANES, (c + 1) * LANES)
        dst[:, cols] = src[cols, :].T.astype(BF16)


def finish(result, out_hbm, qg_hbm, kg_hbm, vg_hbm, sems):
    copies = [pltpu.make_async_copy(result.at[:, a:b], dst, sems.at[i])
              for i, ((a, b), dst) in enumerate(zip(SPANS, (out_hbm, qg_hbm, kg_hbm, vg_hbm)))]
    for copy in copies:
        copy.start()
    for copy in copies:
        copy.wait()


def on_device(q, k, v, do, gain):
    n = lax.axis_size("seq")
    chips = n // 2
    rows = -(-PACKED // (16 * chips)) * 16
    vm = pltpu.VMEM

    def both(*shape, dtype=BF16):
        return vm((2,) + shape, dtype)

    packed = vm((PACKED, LANES), BF16)
    ring = vm((chips * rows, LANES), BF16)
    small = vm((chips // 2 * rows, LANES), BF16)
    rim = vm(((QW + VW) // 2, LANES), BF16)
    result = pl.pallas_call(
        functools.partial(whole, n, rows),
        out_shape=pltpu.VMEM((BLK, SPANS[-1][1]), BF16),
        in_specs=[pl.BlockSpec(memory_space=pltpu.HBM)] * 5,
        out_specs=pl.BlockSpec(memory_space=vm),
        scratch_shapes=[
            vm((BLK, QW), BF16), vm((BLK, VW), BF16), vm((BLK, QW), BF16), vm((BLK, VW), BF16),
            vm((BLK, QW), BF16), vm((BLK, VW), BF16), vm((H * DV // LANES, LANES), F32),
            pltpu.SemaphoreType.DMA((9,)),
            vm((QW, BLK), BF16), vm((VW, BLK), BF16), packed,
            both(PACKED, LANES), ring, ring, small, ring, packed, both(PACKED, LANES),
            both(PACKED, LANES), ring, ring, small, ring, packed, both(PACKED, LANES),
            rim, rim, vm((BLK, QW), BF16), vm((BLK, VW), BF16),
            both(QW, BLK), both(VW, BLK), both(VW, BLK), both(VW, BLK),
            both(VW, BLK, dtype=F32), both(VW, BLK, dtype=F32), both(QW, BLK, dtype=F32),
            both(QW, 384, dtype=F32), both(VW, 384, dtype=F32), both(QW, BLK, dtype=F32),
            both(384, QW), both(384, VW), both(QW, 384), both(VW, 384),
            vm((VW, LANES), F32),
            vm((BLK, VW), BF16), vm((BLK, QW), BF16), vm((BLK, QW), BF16), vm((BLK, VW), BF16),
            both(QW, BLK), both(VW, BLK),
            pltpu.SemaphoreType.DMA((4, chips)), pltpu.SemaphoreType.DMA((4, chips)),
            pltpu.SemaphoreType.DMA((2,)), pltpu.SemaphoreType.DMA((2,)),
            pltpu.SemaphoreType.DMA((9,)), pltpu.SemaphoreType.DMA((9,)),
            pltpu.SemaphoreType.DMA((5,)), pltpu.SemaphoreType.DMA((3,)),
        ],
        compiler_params=pltpu.CompilerParams(
            vmem_limit_bytes=24 * 1024 * 1024, collective_id=0, has_side_effects=True),
    )(*(pltpu.with_memory_space_constraint(x, pltpu.HBM)
        for x in (q, k, v, do, gain.reshape(H * DV // LANES, LANES))))
    return pl.pallas_call(
        finish,
        out_shape=[jax.ShapeDtypeStruct(x.shape, BF16) for x in (do, q, k, v)],
        in_specs=[pl.BlockSpec(memory_space=vm)],
        out_specs=[pl.BlockSpec(memory_space=pltpu.HBM)] * 4,
        scratch_shapes=[pltpu.SemaphoreType.DMA((4,))],
        compiler_params=pltpu.CompilerParams(vmem_limit_bytes=1024 * 1024),
    )(result)


def solution(mesh):
    split = P(("groups", "seq"), None)
    return jax.shard_map(
        on_device, mesh=mesh, in_specs=(split,) * 4 + (P(),), out_specs=(split,) * 4, check_vma=False
    )
```

```python
import functools

import jax
import jax.numpy as jnp
from jax import lax
from jax.experimental import pallas as pl
from jax.experimental.pallas import tpu as pltpu
from jax.sharding import PartitionSpec as P

H = 16
FD = 16
DV = 64
WIN = 64
BLK = 256
LANES = 128
HC = H // 2
QW = HC * FD
VW = HC * DV
PACKED = VW + VW // 4
QUAD = 0.17677669529663687
EPS = 1e-06
NEG = -1e30
SPANS = ((0, H * DV), (H * DV, H * (DV + FD)), (H * (DV + FD), H * (DV + 2 * FD)), (H * (DV + 2 * FD), H * 2 * (DV + FD)))
F32 = jnp.float32
BF16 = jnp.bfloat16

NN = (((1,), (0,)), ((), ()))
NT = (((1,), (1,)), ((), ()))
TN = (((0,), (0,)), ((), ()))


def mm(a, b, dims=NN):
    return lax.dot_general(a, b, dims, preferred_element_type=F32)


def features(x):
    parts = [x * x * QUAD]
    for d in range(1, 8):
        parts.append(x * pltpu.roll(x, FD - d, 0) * 0.25)
    parts.append(x[:8] * x[8:] * 0.25)
    row = lax.broadcasted_iota(jnp.int32, (8, x.shape[1]), 0)
    parts.append(jnp.where(row == 0, 1.0, 0.0).astype(F32))
    parts.append(x * 0.5)
    return jnp.concatenate(parts, axis=0).astype(BF16)


def features_back(g, x):
    dx = (2.0 * QUAD) * g[:FD] * x
    for d in range(1, 8):
        part = g[d * FD : (d + 1) * FD] * 0.25
        dx = dx + part * pltpu.roll(x, FD - d, 0) + pltpu.roll(part * x, d, 0)
    half = g[128:136] * 0.25
    dx = dx + jnp.concatenate([half * x[8:], half * x[:8]], axis=0)
    return dx + 0.5 * g[144:160]


def turn(dst, src):
    for c in range(src.shape[1] // LANES):
        cols = slice(c * LANES, (c + 1) * LANES)
        dst[cols, :] = src[:, cols].T


def put_state(buf, group, states):
    for i, st in enumerate(states):
        at = group * 256 + i * 64
        buf[at : at + 64, :] = st[:, :128].astype(BF16)
    rest = jnp.concatenate([st[:, 128:160] for st in states], axis=1)
    buf[VW + group * 64 : VW + group * 64 + 64, :] = rest.astype(BF16)


def get_state(buf, group, i):
    at = group * 256 + i * 64
    main = buf[at : at + 64, :]
    rest = buf[VW + group * 64 : VW + group * 64 + 64, :][:, i * 32 : (i + 1) * 32]
    return main, rest


def qk_rows(h):
    return pl.ds(pl.multiple_of(h * FD, FD), FD) if not isinstance(h, int) else slice(h * FD, (h + 1) * FD)


def v_rows(h):
    return pl.ds(pl.multiple_of(h * DV, DV), DV) if not isinstance(h, int) else slice(h * DV, (h + 1) * DV)


def head_mask(rows, width, which):
    row = lax.broadcasted_iota(jnp.int32, (128, rows), 0)
    return (row >= which * width) & (row < (which + 1) * width)


def tile_scores(kx, q_all, head):
    zero = jnp.zeros_like(q_all)
    picked = jnp.where(head_mask(q_all.shape[1], FD, head), q_all, zero)
    return mm(kx, picked) * 0.25


def kernel_mask():
    r = lax.broadcasted_iota(jnp.int32, (128, 128), 0)
    c = lax.broadcasted_iota(jnp.int32, (128, 128), 1)
    return r <= c


def stage_state(kt, vt, state):
    for group in range(HC // 4):
        states = []
        for i in range(4):
            h = group * 4 + i
            phi = features(kt[qk_rows(h), :].astype(F32))
            states.append(mm(vt[v_rows(h), :], phi, NT))
        put_state(state, group, states)


def masked_quads(full, below):
    zero = jnp.zeros((128, 128), F32)
    top = jnp.concatenate([jnp.where(below, full[:128, :128], 0.0), full[:128, 128:]], axis=1)
    low = jnp.concatenate([zero, jnp.where(below, full[128:, 128:], 0.0)], axis=1)
    return jnp.concatenate([top, low], axis=0).astype(BF16)


def stage_num(qt_ref, num_ref, kx, vtx):
    below = kernel_mask()

    @pl.loop(0, HC // 2)
    def _(pair):
        for i in range(2):
            h = pair * 2 + i
            s = tile_scores(kx[128:384, :], qt_ref[...], h)
            kern = masked_quads(1.0 + s + 0.5 * s * s, below)
            num_ref[v_rows(h), :] = mm(vtx[v_rows(h), 128:384], kern)


def stage_win(lo, hi, first, qt_ref, dot_ref, win_ref, dq_ref, dk_ref, dv_ref, kx, vx, ktx, vtx):
    r = lax.broadcasted_iota(jnp.int32, (192, 256), 0)
    c = lax.rem(lax.broadcasted_iota(jnp.int32, (192, 256), 1), 128)
    band = (r >= c + 1) & (r <= c + 64)
    band0 = band if first is None else band & (r >= jnp.where(first, 64, 0))
    halves = [head_mask(128, DV, i) for i in range(2)]

    @pl.loop(lo, hi)
    def _(pair):
        prow = pl.ds(pl.multiple_of(pair * LANES, LANES), LANES)
        dks = [[], []]
        dvs = [[], []]
        for j in range(2):
            cols = slice(j * 128, (j + 1) * 128)
            keys = slice(j * 128, j * 128 + 256)
            near = slice(j * 128 + 64, j * 128 + 256)
            q_all = qt_ref[:, cols]
            zero = jnp.zeros_like(q_all)
            picked = jnp.concatenate(
                [jnp.where(head_mask(LANES, FD, pair * 2 + i), q_all, zero) for i in range(2)], axis=1)
            s = mm(kx[near, :], picked) * 0.25
            sw = jnp.where(band0 if j == 0 else band, s, NEG)
            e = jnp.exp(sw - jnp.max(sw, axis=0, keepdims=True))
            p = e * (1.0 / jnp.sum(e, axis=0, keepdims=True))
            do_pair = dot_ref[prow, cols]
            do_both = jnp.concatenate([jnp.where(m, do_pair, jnp.zeros_like(do_pair)) for m in halves], axis=1)
            dw = mm(vx[near, prow], do_both)
            ds = p * (dw - jnp.sum(p * dw, axis=0, keepdims=True)) * 0.25
            pad = jnp.zeros((64, 256), BF16)
            ds = jnp.concatenate([pad, ds.astype(BF16)], axis=0)
            wide = jnp.concatenate([pad, p.astype(BF16)], axis=0)
            for i in range(2):
                h = pair * 2 + i
                ds_one = ds[:, i * 128 : (i + 1) * 128]
                wide_one = wide[:, i * 128 : (i + 1) * 128]
                win_ref[v_rows(h), cols] = mm(vtx[v_rows(h), keys], wide_one)
                dq_ref[qk_rows(h), cols] = mm(ktx[qk_rows(h), keys], ds_one)
                dks[i].append(mm(qt_ref[qk_rows(h), cols], ds_one, NT))
                dvs[i].append(mm(dot_ref[v_rows(h), cols], wide_one, NT))
        for i in range(2):
            h = pair * 2 + i
            for dst, rows, parts in ((dk_ref, qk_rows(h), dks[i]), (dv_ref, v_rows(h), dvs[i])):
                dst[rows, 0:128] = parts[0][:, :128]
                dst[rows, 128:256] = parts[0][:, 128:] + parts[1][:, :128]
                dst[rows, 256:384] = parts[1][:, 128:]


def stage_mix(prefix_ref, qt_ref, dot_ref, num_ref, gain_ref, dnum_ref, state_ref):
    for group in range(HC // 4):
        states = []
        for i in range(4):
            h = group * 4 + i
            phi = features(qt_ref[qk_rows(h), :].astype(F32))
            main, rest = get_state(prefix_ref, group, i)
            num = num_ref[v_rows(h), :] + mm(main, phi[:128]) + mm(rest, phi[128:])
            inv = lax.rsqrt(jnp.mean(num * num, axis=0, keepdims=True) + EPS)
            gain = jnp.concatenate([gain_ref[v_rows(h), :]] * 2, axis=1)
            unit = num * inv
            num_ref[v_rows(h), :] = unit * gain
            dg = dot_ref[v_rows(h), :].astype(F32) * gain
            dnum = inv * (dg - unit * jnp.mean(dg * unit, axis=0, keepdims=True))
            half = dnum.astype(BF16)
            dnum_ref[v_rows(h), :] = half
            states.append(mm(half, phi, NT))
        put_state(state_ref, group, states)


def stage_back(lo, hi, prefix_ref, qt_ref, kt_ref, k_ref, v_ref, dnum_ref, dqt, dkb, dvb):
    below = kernel_mask()

    @pl.loop(lo, hi)
    def _(group):
        for i in range(4):
            h = group * 4 + i
            pcol = pl.ds(pl.multiple_of((group * 2 + i // 2) * LANES, LANES), LANES)
            main = prefix_ref[v_rows(h), :]
            rest = prefix_ref[pl.ds(pl.multiple_of(VW + group * 64, 64), 64), :][:, i * 32 : (i + 1) * 32]
            dnum = dnum_ref[v_rows(h), :]
            dphi = jnp.concatenate([mm(main, dnum, TN), mm(rest, dnum, TN)], axis=0)
            dq = features_back(dphi, qt_ref[qk_rows(h), :].astype(F32))
            s = tile_scores(k_ref[...], qt_ref[...], h)
            dn_pair = dnum_ref[pcol, :]
            dn_one = jnp.where(head_mask(BLK, DV, i % 2), dn_pair, jnp.zeros_like(dn_pair))
            dkern = mm(v_ref[:, pcol], dn_one)
            kern = masked_quads(1.0 + s + 0.5 * s * s, below)
            ds = masked_quads(dkern * (0.25 + 0.25 * s), below)
            dqt[qk_rows(h), :] = dq + mm(kt_ref[qk_rows(h), :], ds)
            dkb[qk_rows(h), :] = mm(qt_ref[qk_rows(h), :], ds, NT)
            dvb[v_rows(h), :] = mm(dnum, kern, NT)


def stage_last(suffix_ref, kt_ref, vt_ref, dk_in, dv_in, dkb, dvb, dkt, dvt):
    for group in range(HC // 4):
        for i in range(4):
            h = group * 4 + i
            main, rest = get_state(suffix_ref, group, i)
            x = kt_ref[qk_rows(h), :].astype(F32)
            phi = features(x)
            vt = vt_ref[v_rows(h), :]
            dv = dv_in[v_rows(h), :] + dvb[v_rows(h), :] + mm(main, phi[:128]) + mm(rest, phi[128:])
            dphi = jnp.concatenate([mm(main, vt, TN), mm(rest, vt, TN)], axis=0)
            dk = dk_in[qk_rows(h), :] + dkb[qk_rows(h), :] + features_back(dphi, x)
            dkt[qk_rows(h), :] = dk.astype(BF16)
            dvt[v_rows(h), :] = dv.astype(BF16)


def whole(n, rows, q_hbm, k_hbm, v_hbm, do_hbm, gain_hbm, res,
          k_far, v_far, q_far, do_far, q_own, do_own, gain_in, load_sem,
          kt_o, vt_o, st_out, st2, sum1, got1, send2, base1, near1, prefix,
          dst2, sum3, got3, send4, base3, near3, suffix, rim_out, rim_in,
          qx, dox, qt, dot, dnum, num, win, dq, dk, dv, dkb, dvb, dqt, kx, vx, ktx, vtx, gain,
          out_o, qg_o, kg_o, vg_o, dkt, dvt,
          send_sem, recv_sem, near_send, near_recv, pair_send, pair_recv, rim_send, rim_recv):
    me = lax.axis_index("seq")
    out_ref, qg_ref, kg_ref, vg_ref = (res.at[:, a:b] for a, b in SPANS)
    chips = n // 2
    planes = chips // 2
    chip = me // 2
    core = lax.rem(me, 2)
    far = 1 - core
    other = chip * 2 + far
    odd = lax.rem(chip, 2)
    barrier = pltpu.get_barrier_semaphore()

    def greet(to):
        pl.semaphore_signal(barrier, inc=1, device_id={"seq": to}, device_id_type=pl.DeviceIdType.MESH)

    @pl.loop(0, chips)
    def _(step):
        j = jnp.where(chip >= planes, step, chips - 1 - step)

        @pl.when(j != chip)
        def _():
            greet(j * 2 + core)

    greet(other)

    def load(index, src, dst):
        copy = pltpu.make_async_copy(src, dst, load_sem.at[index])
        copy.start()
        return copy

    def columns(which, width):
        return pl.ds(pl.multiple_of(which * width, LANES), width)

    loads = [load(i, src.at[:, columns(which, w)], dst) for i, (src, which, w, dst) in enumerate((
        (k_hbm, far, QW, k_far), (v_hbm, far, VW, v_far),
        (k_hbm, core, QW, kx.at[core, 128:384, :]), (v_hbm, core, VW, vx.at[core, 128:384, :]),
        (q_hbm, far, QW, q_far), (do_hbm, far, VW, do_far),
        (q_hbm, core, QW, q_own), (do_hbm, core, VW, do_own)))]
    loads.append(load(8, gain_hbm, gain_in))

    def remote(src, dst, ssem, rsem, to):
        return pltpu.make_async_remote_copy(
            src_ref=src, dst_ref=dst, send_sem=ssem, recv_sem=rsem,
            device_id={"seq": to}, device_id_type=pl.DeviceIdType.MESH)

    def chunk(ref, i):
        return ref.at[pl.ds(pl.multiple_of(i * rows, 16), rows), :]

    def cut(which, width):
        return pl.ds(pl.multiple_of(which * width, LANES), width)

    def pair_copy(index, src, dst):
        return remote(src, dst, pair_send.at[index], pair_recv.at[index], other)

    def is_in(span):
        return (chip >= span[0]) & (chip < span[1])

    def over(span, reach, body):
        lo, hi = span

        @pl.loop(lo, hi)
        def _(step):
            j = jnp.where(chip >= planes, step, lo + hi - 1 - step)

            @pl.when(j != chip)
            def _():
                body(j)

    def gather_copy(phase, src, dst, j):
        return remote(chunk(src, j), chunk(dst, chip), send_sem.at[phase, j], recv_sem.at[phase, chip], j * 2 + core)

    def gather_start(phase, span, src, dst):
        @pl.when(is_in(span))
        def _():
            over((0, chips), None, lambda j: gather_copy(phase, src, dst, j).start())

        chunk(dst, chip)[...] = chunk(src, chip)[...]

    def gather_wait(phase, span, src, dst):
        over(span, None, lambda j: remote(
            chunk(src, j), chunk(dst, j), send_sem.at[phase, j], recv_sem.at[phase, j], j * 2 + core).wait_recv())

        @pl.when(is_in(span))
        def _():
            over((0, chips), None, lambda j: gather_copy(phase, src, dst, j).wait_send())

    def spread_copy(phase, src, dst, j):
        return remote(chunk(src, j // 2), chunk(dst, chip), send_sem.at[phase, j], recv_sem.at[phase, chip],
                      j * 2 + core)

    def spread_start(phase, span, src, dst):
        over(span, None, lambda j: spread_copy(phase, src, dst, j).start())

        @pl.when(is_in(span))
        def _():
            chunk(dst, chip)[...] = chunk(src, chip // 2)[...]

        @pl.when(jnp.logical_not(is_in(span)))
        def _():
            dst[...] = jnp.zeros_like(dst)

    def spread_wait(phase, span, src, dst):
        @pl.when(is_in(span))
        def _():
            over((0, chips), None, lambda j: remote(
                chunk(src, j // 2), chunk(dst, j), send_sem.at[phase, j], recv_sem.at[phase, j],
                j * 2 + core).wait_recv())

        over(span, None, lambda j: spread_copy(phase, src, dst, j).wait_send())

    def near_copy(index, src, dst, to):
        return remote(src.at[0:PACKED, :], dst, near_send.at[index], near_recv.at[index], to * 2 + core)

    def scan(src, dst, reverse):
        def step(i, total):
            p = planes - 1 - i if reverse else i
            chunk(dst, p)[...] = total.astype(BF16)
            return total + (chunk(src, 2 * p)[...].astype(F32) + chunk(src, 2 * p + 1)[...].astype(F32))

        total = lax.fori_loop(0, planes - 1, step, jnp.zeros((rows, LANES), F32))
        chunk(dst, 0 if reverse else planes - 1)[...] = total.astype(BF16)

    def chip_sum(src, dst):
        dst[0:PACKED, :] = (src[0].astype(F32) + src[1].astype(F32)).astype(BF16)
        if chips * rows > PACKED:
            dst[PACKED:, :] = jnp.zeros((chips * rows - PACKED, LANES), BF16)

    early, late = (0, chips - 2), (2, chips)
    first_chip = chip == 0
    end_chip = chip == chips - 1
    after = jnp.minimum(chip + 1, chips - 1)
    before = jnp.maximum(chip - 1, 0)

    kt_own = ktx.at[core, :, 128:384]
    vt_own = vtx.at[core, :, 128:384]
    loads[0].wait()
    turn(kt_o, k_far)
    loads[1].wait()
    turn(vt_o, v_far)
    stage_state(kt_o, vt_o, st_out)
    def number(b):
        stage_num(*(r.at[b] for r in (qt, num, kx, vtx)))

    pl.semaphore_wait(barrier, chips)

    state_copy = pair_copy(0, st_out, st2.at[core])
    state_copy.start()
    loads[2].wait()
    turn(kt_own, kx.at[core, 128:384, :])
    loads[3].wait()
    turn(vt_own, vx.at[core, 128:384, :])
    stage_state(kt_own, vt_own, st2.at[core])
    token_copies = [
        pair_copy(1, k_far, kx.at[core, 128:384, :]),
        pair_copy(2, v_far, vx.at[core, 128:384, :]),
        pair_copy(3, q_far, qx),
        pair_copy(4, do_far, dox),
    ]
    pair_copy(0, st_out, st2.at[far]).wait_recv()
    chip_sum(st2, sum1)
    gather_start(0, early, sum1, got1)

    @pl.when(odd == 0)
    def _():
        near_copy(0, sum1, near1, chip + 1).start()

    def rim_copies():
        return [remote(src.at[1, 320:384, :], src.at[0, 64:128, :], rim_send.at[m], rim_recv.at[m], after * 2 + core)
                for m, src in enumerate((kx, vx))]

    loads[4].wait()
    loads[5].wait()
    for copy in token_copies:
        copy.start()
    state_copy.wait_send()
    for copy in loads[6:]:
        copy.wait()
    turn(qt.at[core], q_own)
    turn(dot.at[core], do_own)
    kx[0, 0:64, :] = jnp.zeros((64, QW), BF16)
    vx[0, 0:64, :] = jnp.zeros((64, VW), BF16)

    @pl.when(first_chip)
    def _():
        kx[0, 64:128, :] = jnp.zeros((64, QW), BF16)
        vx[0, 64:128, :] = jnp.zeros((64, VW), BF16)

    for c in range(VW // LANES):
        row = gain_in[pl.ds(core * (VW // LANES) + c, 1), :]
        gain[c * LANES : (c + 1) * LANES, :] = jnp.broadcast_to(row, (LANES, LANES)).T
    number(core)
    for copy in token_copies:
        copy.wait_send()
    arrivals = [
        pair_copy(1, k_far, kx.at[far, 128:384, :]),
        pair_copy(2, v_far, vx.at[far, 128:384, :]),
        token_copies[2], token_copies[3],
    ]
    for copy in arrivals:
        copy.wait_recv()
    turn(ktx.at[far, :, 128:384], kx.at[far, 128:384, :])
    turn(vtx.at[far, :, 128:384], vx.at[far, 128:384, :])
    turn(qt.at[far], qx)
    turn(dot.at[far], dox)
    kx[1, 0:128, :] = kx[0, 256:384, :]
    vx[1, 0:128, :] = vx[0, 256:384, :]
    ktx[1, :, 0:128] = ktx[0, :, 256:384]
    vtx[1, :, 0:128] = vtx[0, :, 256:384]

    @pl.when(jnp.logical_not(end_chip))
    def _():
        for copy in rim_copies():
            copy.start()

    def window(b, lo, hi):
        stage_win(lo, hi, first_chip if b == 0 else None, *(r.at[b] for r in (
            qt, dot, win, dq, dk, dv, kx, vx, ktx, vtx)))

    number(far)
    window(1, 0, 2)
    gather_wait(0, early, sum1, got1)
    scan(got1, send2, False)
    spread_start(1, late, send2, base1)
    window(1, 2, 4)

    @pl.when(jnp.logical_not(first_chip))
    def _():
        for copy in rim_copies():
            copy.wait_recv()

    @pl.when(jnp.logical_not(end_chip))
    def _():
        for copy in rim_copies():
            copy.wait_send()

    turn(ktx.at[0, :, 0:128], kx.at[0, 0:128, :])
    turn(vtx.at[0, :, 0:128], vx.at[0, 0:128, :])
    window(0, 0, 2)

    @pl.when(odd == 1)
    def _():
        near_copy(0, sum1, near1, chip).wait_recv()

    @pl.when(odd == 0)
    def _():
        near_copy(0, sum1, near1, chip + 1).wait_send()
        near1[...] = jnp.zeros_like(near1)

    spread_wait(1, late, send2, base1)

    def bases(base, near, state, dst, order):
        total = base[0:PACKED, :].astype(F32) + near[...].astype(F32)
        dst[order[0]] = total.astype(BF16)
        dst[order[1]] = (total + state[order[0]].astype(F32)).astype(BF16)

    bases(base1, near1, st2, prefix, (0, 1))
    for b in range(2):
        stage_mix(*(r.at[b] for r in (prefix, qt, dot, num)), gain, dnum.at[b], dst2.at[b])

    chip_sum(dst2, sum3)
    gather_start(2, late, sum3, got3)

    @pl.when(odd == 1)
    def _():
        near_copy(1, sum3, near3, chip - 1).start()

    window(0, 2, 4)

    for ref, at, lo in ((dk, 0, 0), (dv, QW, QW)):
        size = ref.shape[1] // 2
        top = ref[0, 0:size, 0:128]
        rim_out[lo // 2 : lo // 2 + size, :] = (pltpu.roll(top, 64, 1) + ref[0, size : 2 * size, 0:128]).astype(BF16)

    def rim_back(to):
        return remote(rim_out, rim_in, rim_send.at[2], rim_recv.at[2], to * 2 + core)

    @pl.when(jnp.logical_not(first_chip))
    def _():
        rim_back(before).start()

    def back(b, lo, hi):
        stage_back(lo, hi, *(r.at[b] for r in (prefix, qt)), ktx.at[b, :, 128:384], kx.at[b, 128:384, :],
                   vx.at[b, 128:384, :], *(r.at[b] for r in (dnum, dqt, dkb, dvb)))

    back(0, 0, 1)
    gather_wait(2, late, sum3, got3)
    scan(got3, send4, True)
    spread_start(3, early, send4, base3)
    turn_sum(out_o, num.at[far], win.at[far])
    out_copy = pair_copy(5, out_o, out_ref.at[:, cut(core, VW)])
    out_copy.start()
    turn_sum(out_ref.at[:, cut(core, VW)], num.at[core], win.at[core])
    back(0, 1, 2)
    back(1, 0, 2)
    turn_sum(qg_o, dqt.at[far], dq.at[far])
    qg_copy = pair_copy(6, qg_o, qg_ref.at[:, cut(core, QW)])
    qg_copy.start()
    turn_sum(qg_ref.at[:, cut(core, QW)], dqt.at[core], dq.at[core])

    @pl.when(end_chip)
    def _():
        rim_in[...] = jnp.zeros_like(rim_in)

    @pl.when(jnp.logical_not(end_chip))
    def _():
        rim_back(after).wait_recv()

    @pl.when(jnp.logical_not(first_chip))
    def _():
        rim_back(before).wait_send()

    for ref, lo in ((dk, 0), (dv, QW)):
        size = ref.shape[1] // 2
        ref[0, :, 256:384] = ref[0, :, 256:384] + ref[1, :, 0:128]
        got = rim_in[lo // 2 : lo // 2 + size, :].astype(F32)
        upper = lax.broadcasted_iota(jnp.int32, got.shape, 1) >= 64
        zero = jnp.zeros_like(got)
        ref[1, 0:size, 256:384] = ref[1, 0:size, 256:384] + jnp.where(upper, pltpu.roll(got, 64, 1), zero)
        ref[1, size : 2 * size, 256:384] = ref[1, size : 2 * size, 256:384] + jnp.where(upper, got, zero)

    @pl.when(odd == 0)
    def _():
        near_copy(1, sum3, near3, chip).wait_recv()

    @pl.when(odd == 1)
    def _():
        near_copy(1, sum3, near3, chip - 1).wait_send()
        near3[...] = jnp.zeros_like(near3)

    spread_wait(3, early, send4, base3)
    bases(base3, near3, dst2, suffix, (1, 0))

    def last(b, dk_to, dv_to):
        stage_last(suffix.at[b], ktx.at[b, :, 128:384], vtx.at[b, :, 128:384],
                   dk.at[b, :, 128:384], dv.at[b, :, 128:384], dkb.at[b], dvb.at[b], dk_to, dv_to)

    last(far, dkt.at[0], dvt.at[0])
    turn_out(kg_o, dkt.at[0])
    turn_out(vg_o, dvt.at[0])
    ends = [pair_copy(7, kg_o, kg_ref.at[:, cut(core, QW)]), pair_copy(8, vg_o, vg_ref.at[:, cut(core, VW)])]
    for copy in ends:
        copy.start()
    last(core, dkt.at[1], dvt.at[1])
    turn_out(kg_ref.at[:, cut(core, QW)], dkt.at[1])
    turn_out(vg_ref.at[:, cut(core, VW)], dvt.at[1])
    returns = [
        pair_copy(5, out_o, out_ref.at[:, cut(far, VW)]), pair_copy(6, qg_o, qg_ref.at[:, cut(far, QW)]),
        pair_copy(7, kg_o, kg_ref.at[:, cut(far, QW)]), pair_copy(8, vg_o, vg_ref.at[:, cut(far, VW)]),
    ]
    for copy in returns:
        copy.wait_recv()
        copy.wait_send()


def turn_out(dst, src):
    for c in range(dst.shape[1] // LANES):
        cols = slice(c * LANES, (c + 1) * LANES)
        dst[:, cols] = src[cols, :].T.astype(BF16)


def turn_sum(dst, one, two):
    for c in range(dst.shape[1] // LANES):
        cols = slice(c * LANES, (c + 1) * LANES)
        dst[:, cols] = (one[cols, :] + two[cols, :]).astype(BF16).T


def finish(result, out_hbm, qg_hbm, kg_hbm, vg_hbm, sems):
    copies = [pltpu.make_async_copy(result.at[:, a:b], dst, sems.at[i])
              for i, ((a, b), dst) in enumerate(zip(SPANS, (out_hbm, qg_hbm, kg_hbm, vg_hbm)))]
    for copy in copies:
        copy.start()
    for copy in copies:
        copy.wait()


def on_device(q, k, v, do, gain):
    n = lax.axis_size("seq")
    chips = n // 2
    rows = -(-PACKED // (16 * chips)) * 16
    vm = pltpu.VMEM

    def both(*shape, dtype=BF16):
        return vm((2,) + shape, dtype)

    packed = vm((PACKED, LANES), BF16)
    ring = vm((chips * rows, LANES), BF16)
    small = vm((chips // 2 * rows, LANES), BF16)
    rim = vm(((QW + VW) // 2, LANES), BF16)
    result = pl.pallas_call(
        functools.partial(whole, n, rows),
        out_shape=pltpu.VMEM((BLK, SPANS[-1][1]), BF16),
        in_specs=[pl.BlockSpec(memory_space=pltpu.HBM)] * 5,
        out_specs=pl.BlockSpec(memory_space=vm),
        scratch_shapes=[
            vm((BLK, QW), BF16), vm((BLK, VW), BF16), vm((BLK, QW), BF16), vm((BLK, VW), BF16),
            vm((BLK, QW), BF16), vm((BLK, VW), BF16), vm((H * DV // LANES, LANES), F32),
            pltpu.SemaphoreType.DMA((9,)),
            vm((QW, BLK), BF16), vm((VW, BLK), BF16), packed,
            both(PACKED, LANES), ring, ring, small, ring, packed, both(PACKED, LANES),
            both(PACKED, LANES), ring, ring, small, ring, packed, both(PACKED, LANES),
            rim, rim, vm((BLK, QW), BF16), vm((BLK, VW), BF16),
            both(QW, BLK), both(VW, BLK), both(VW, BLK),
            both(VW, BLK, dtype=F32), both(VW, BLK, dtype=F32), both(QW, BLK, dtype=F32),
            both(QW, 384, dtype=F32), both(VW, 384, dtype=F32),
            both(QW, BLK, dtype=F32), both(VW, BLK, dtype=F32), both(QW, BLK, dtype=F32),
            both(384, QW), both(384, VW), both(QW, 384), both(VW, 384),
            vm((VW, LANES), F32),
            vm((BLK, VW), BF16), vm((BLK, QW), BF16), vm((BLK, QW), BF16), vm((BLK, VW), BF16),
            both(QW, BLK), both(VW, BLK),
            pltpu.SemaphoreType.DMA((4, chips)), pltpu.SemaphoreType.DMA((4, chips)),
            pltpu.SemaphoreType.DMA((2,)), pltpu.SemaphoreType.DMA((2,)),
            pltpu.SemaphoreType.DMA((9,)), pltpu.SemaphoreType.DMA((9,)),
            pltpu.SemaphoreType.DMA((3,)), pltpu.SemaphoreType.DMA((3,)),
        ],
        compiler_params=pltpu.CompilerParams(
            vmem_limit_bytes=24 * 1024 * 1024, collective_id=0, has_side_effects=True),
    )(*(pltpu.with_memory_space_constraint(x, pltpu.HBM)
        for x in (q, k, v, do, gain.reshape(H * DV // LANES, LANES))))
    return pl.pallas_call(
        finish,
        out_shape=[jax.ShapeDtypeStruct(x.shape, BF16) for x in (do, q, k, v)],
        in_specs=[pl.BlockSpec(memory_space=vm)],
        out_specs=[pl.BlockSpec(memory_space=pltpu.HBM)] * 4,
        scratch_shapes=[pltpu.SemaphoreType.DMA((4,))],
        compiler_params=pltpu.CompilerParams(vmem_limit_bytes=1024 * 1024),
    )(result)


def solution(mesh):
    split = P(("groups", "seq"), None)
    return jax.shard_map(
        on_device, mesh=mesh, in_specs=(split,) * 4 + (P(),), out_specs=(split,) * 4, check_vma=False
    )
```

```python
import functools

import jax
import jax.numpy as jnp
from jax import lax
from jax.experimental import pallas as pl
from jax.experimental.pallas import tpu as pltpu
from jax.sharding import PartitionSpec as P

H = 16
FD = 16
DV = 64
WIN = 64
BLK = 256
LANES = 128
HC = H // 2
QW = HC * FD
VW = HC * DV
PACKED = VW + VW // 4
QUAD = 0.17677669529663687
EPS = 1e-06
NEG = -1e30
SPANS = ((0, H * DV), (H * DV, H * (DV + FD)), (H * (DV + FD), H * (DV + 2 * FD)), (H * (DV + 2 * FD), H * 2 * (DV + FD)))
F32 = jnp.float32
BF16 = jnp.bfloat16

NN = (((1,), (0,)), ((), ()))
NT = (((1,), (1,)), ((), ()))
TN = (((0,), (0,)), ((), ()))


def mm(a, b, dims=NN):
    return lax.dot_general(a, b, dims, preferred_element_type=F32)


def features(x):
    parts = [x * x * QUAD]
    for d in range(1, 8):
        parts.append(x * pltpu.roll(x, FD - d, 0) * 0.25)
    parts.append(x[:8] * x[8:] * 0.25)
    row = lax.broadcasted_iota(jnp.int32, (8, x.shape[1]), 0)
    parts.append(jnp.where(row == 0, 1.0, 0.0).astype(F32))
    parts.append(x * 0.5)
    return jnp.concatenate(parts, axis=0).astype(BF16)


def features_back(g, x):
    dx = (2.0 * QUAD) * g[:FD] * x
    for d in range(1, 8):
        part = g[d * FD : (d + 1) * FD] * 0.25
        dx = dx + part * pltpu.roll(x, FD - d, 0) + pltpu.roll(part * x, d, 0)
    half = g[128:136] * 0.25
    dx = dx + jnp.concatenate([half * x[8:], half * x[:8]], axis=0)
    return dx + 0.5 * g[144:160]


def turn(dst, src):
    for c in range(src.shape[1] // LANES):
        cols = slice(c * LANES, (c + 1) * LANES)
        dst[cols, :] = src[:, cols].T


def put_state(buf, group, states):
    for i, st in enumerate(states):
        at = group * 256 + i * 64
        buf[at : at + 64, :] = st[:, :128].astype(BF16)
    rest = jnp.concatenate([st[:, 128:160] for st in states], axis=1)
    buf[VW + group * 64 : VW + group * 64 + 64, :] = rest.astype(BF16)


def get_state(buf, group, i):
    at = group * 256 + i * 64
    main = buf[at : at + 64, :]
    rest = buf[VW + group * 64 : VW + group * 64 + 64, :][:, i * 32 : (i + 1) * 32]
    return main, rest


def qk_rows(h):
    return pl.ds(pl.multiple_of(h * FD, FD), FD) if not isinstance(h, int) else slice(h * FD, (h + 1) * FD)


def v_rows(h):
    return pl.ds(pl.multiple_of(h * DV, DV), DV) if not isinstance(h, int) else slice(h * DV, (h + 1) * DV)


def head_mask(rows, width, which):
    row = lax.broadcasted_iota(jnp.int32, (128, rows), 0)
    return (row >= which * width) & (row < (which + 1) * width)


def tile_scores(kx, q_all, head):
    zero = jnp.zeros_like(q_all)
    picked = jnp.where(head_mask(q_all.shape[1], FD, head), q_all, zero)
    return mm(kx, picked) * 0.25


def kernel_mask():
    r = lax.broadcasted_iota(jnp.int32, (128, 128), 0)
    c = lax.broadcasted_iota(jnp.int32, (128, 128), 1)
    return r <= c


def stage_state(kt, vt, state):
    for group in range(HC // 4):
        states = []
        for i in range(4):
            h = group * 4 + i
            phi = features(kt[qk_rows(h), :].astype(F32))
            states.append(mm(vt[v_rows(h), :], phi, NT))
        put_state(state, group, states)


def masked_quads(full, below):
    zero = jnp.zeros((128, 128), F32)
    top = jnp.concatenate([jnp.where(below, full[:128, :128], 0.0), full[:128, 128:]], axis=1)
    low = jnp.concatenate([zero, jnp.where(below, full[128:, 128:], 0.0)], axis=1)
    return jnp.concatenate([top, low], axis=0).astype(BF16)


def stage_num(qt_ref, num_ref, kx, vtx):
    below = kernel_mask()

    @pl.loop(0, HC // 2)
    def _(pair):
        for i in range(2):
            h = pair * 2 + i
            s = tile_scores(kx[128:384, :], qt_ref[...], h)
            kern = masked_quads(1.0 + s + 0.5 * s * s, below)
            num_ref[v_rows(h), :] = mm(vtx[v_rows(h), 128:384], kern)


def stage_win(lo, hi, first, qt_ref, dot_ref, win_ref, dq_ref, dk_ref, dv_ref, kx, vx, ktx, vtx):
    r = lax.broadcasted_iota(jnp.int32, (192, 256), 0)
    c = lax.rem(lax.broadcasted_iota(jnp.int32, (192, 256), 1), 128)
    band = (r >= c + 1) & (r <= c + 64)
    band0 = band if first is None else band & (r >= jnp.where(first, 64, 0))
    halves = [head_mask(128, DV, i) for i in range(2)]

    @pl.loop(lo, hi)
    def _(pair):
        prow = pl.ds(pl.multiple_of(pair * LANES, LANES), LANES)
        dks = [[], []]
        dvs = [[], []]
        for j in range(2):
            cols = slice(j * 128, (j + 1) * 128)
            keys = slice(j * 128, j * 128 + 256)
            near = slice(j * 128 + 64, j * 128 + 256)
            q_all = qt_ref[:, cols]
            zero = jnp.zeros_like(q_all)
            picked = jnp.concatenate(
                [jnp.where(head_mask(LANES, FD, pair * 2 + i), q_all, zero) for i in range(2)], axis=1)
            s = mm(kx[near, :], picked) * 0.25
            sw = jnp.where(band0 if j == 0 else band, s, NEG)
            e = jnp.exp(sw - jnp.max(sw, axis=0, keepdims=True))
            p = e * (1.0 / jnp.sum(e, axis=0, keepdims=True))
            do_pair = dot_ref[prow, cols]
            do_both = jnp.concatenate([jnp.where(m, do_pair, jnp.zeros_like(do_pair)) for m in halves], axis=1)
            dw = mm(vx[near, prow], do_both)
            ds = p * (dw - jnp.sum(p * dw, axis=0, keepdims=True)) * 0.25
            pad = jnp.zeros((64, 256), BF16)
            ds = jnp.concatenate([pad, ds.astype(BF16)], axis=0)
            wide = jnp.concatenate([pad, p.astype(BF16)], axis=0)
            for i in range(2):
                h = pair * 2 + i
                ds_one = ds[:, i * 128 : (i + 1) * 128]
                wide_one = wide[:, i * 128 : (i + 1) * 128]
                win_ref[v_rows(h), cols] = mm(vtx[v_rows(h), keys], wide_one)
                dq_ref[qk_rows(h), cols] = mm(ktx[qk_rows(h), keys], ds_one)
                dks[i].append(mm(qt_ref[qk_rows(h), cols], ds_one, NT))
                dvs[i].append(mm(dot_ref[v_rows(h), cols], wide_one, NT))
        for i in range(2):
            h = pair * 2 + i
            for dst, rows, parts in ((dk_ref, qk_rows(h), dks[i]), (dv_ref, v_rows(h), dvs[i])):
                dst[rows, 0:128] = parts[0][:, :128]
                dst[rows, 128:256] = parts[0][:, 128:] + parts[1][:, :128]
                dst[rows, 256:384] = parts[1][:, 128:]


def stage_mix(prefix_ref, qt_ref, dot_ref, num_ref, gain_ref, dnum_ref, state_ref):
    for group in range(HC // 4):
        states = []
        for i in range(4):
            h = group * 4 + i
            phi = features(qt_ref[qk_rows(h), :].astype(F32))
            main, rest = get_state(prefix_ref, group, i)
            num = num_ref[v_rows(h), :] + mm(main, phi[:128]) + mm(rest, phi[128:])
            inv = lax.rsqrt(jnp.mean(num * num, axis=0, keepdims=True) + EPS)
            gain = jnp.concatenate([gain_ref[v_rows(h), :]] * 2, axis=1)
            unit = num * inv
            num_ref[v_rows(h), :] = unit * gain
            dg = dot_ref[v_rows(h), :].astype(F32) * gain
            dnum = inv * (dg - unit * jnp.mean(dg * unit, axis=0, keepdims=True))
            half = dnum.astype(BF16)
            dnum_ref[v_rows(h), :] = half
            states.append(mm(half, phi, NT))
        put_state(state_ref, group, states)


def stage_back(lo, hi, prefix_ref, qt_ref, kt_ref, k_ref, v_ref, dnum_ref, dqt, dkb, dvb):
    below = kernel_mask()

    @pl.loop(lo, hi)
    def _(group):
        for i in range(4):
            h = group * 4 + i
            pcol = pl.ds(pl.multiple_of((group * 2 + i // 2) * LANES, LANES), LANES)
            main = prefix_ref[v_rows(h), :]
            rest = prefix_ref[pl.ds(pl.multiple_of(VW + group * 64, 64), 64), :][:, i * 32 : (i + 1) * 32]
            dnum = dnum_ref[v_rows(h), :]
            dphi = jnp.concatenate([mm(main, dnum, TN), mm(rest, dnum, TN)], axis=0)
            dq = features_back(dphi, qt_ref[qk_rows(h), :].astype(F32))
            s = tile_scores(k_ref[...], qt_ref[...], h)
            dn_pair = dnum_ref[pcol, :]
            dn_one = jnp.where(head_mask(BLK, DV, i % 2), dn_pair, jnp.zeros_like(dn_pair))
            dkern = mm(v_ref[:, pcol], dn_one)
            kern = masked_quads(1.0 + s + 0.5 * s * s, below)
            ds = masked_quads(dkern * (0.25 + 0.25 * s), below)
            dqt[qk_rows(h), :] = dq + mm(kt_ref[qk_rows(h), :], ds)
            dkb[qk_rows(h), :] = mm(qt_ref[qk_rows(h), :], ds, NT)
            dvb[v_rows(h), :] = mm(dnum, kern, NT)


def stage_last(suffix_ref, kt_ref, vt_ref, dk_in, dv_in, dkb, dvb, dkt, dvt):
    for group in range(HC // 4):
        for i in range(4):
            h = group * 4 + i
            main, rest = get_state(suffix_ref, group, i)
            x = kt_ref[qk_rows(h), :].astype(F32)
            phi = features(x)
            vt = vt_ref[v_rows(h), :]
            dv = dv_in[v_rows(h), :] + dvb[v_rows(h), :] + mm(main, phi[:128]) + mm(rest, phi[128:])
            dphi = jnp.concatenate([mm(main, vt, TN), mm(rest, vt, TN)], axis=0)
            dk = dk_in[qk_rows(h), :] + dkb[qk_rows(h), :] + features_back(dphi, x)
            dkt[qk_rows(h), :] = dk.astype(BF16)
            dvt[v_rows(h), :] = dv.astype(BF16)


def whole(n, rows, q_hbm, k_hbm, v_hbm, do_hbm, gain_hbm, res,
          k_far, v_far, q_far, do_far, q_own, do_own, gain_in, load_sem,
          kt_o, vt_o, st_out, st2, sum1, got1, send2, base1, near1, prefix,
          dst2, sum3, got3, send4, base3, near3, suffix, rim_out, rim_in,
          qx, dox, qt, dot, dnum, num, win, dq, dk, dv, dkb, dvb, dqt, kx, vx, ktx, vtx, gain,
          out_o, qg_o, kg_o, vg_o, dkt, dvt,
          send_sem, recv_sem, near_send, near_recv, pair_send, pair_recv, rim_send, rim_recv):
    me = lax.axis_index("seq")
    out_ref, qg_ref, kg_ref, vg_ref = (res.at[:, a:b] for a, b in SPANS)
    chips = n // 2
    planes = chips // 2
    chip = me // 2
    core = lax.rem(me, 2)
    far = 1 - core
    other = chip * 2 + far
    odd = lax.rem(chip, 2)
    barrier = pltpu.get_barrier_semaphore()

    def greet(to):
        pl.semaphore_signal(barrier, inc=1, device_id={"seq": to}, device_id_type=pl.DeviceIdType.MESH)

    @pl.loop(0, chips)
    def _(step):
        j = jnp.where(chip >= planes, step, chips - 1 - step)

        @pl.when(j != chip)
        def _():
            greet(j * 2 + core)

    greet(other)

    def load(index, src, dst):
        copy = pltpu.make_async_copy(src, dst, load_sem.at[index])
        copy.start()
        return copy

    def columns(which, width):
        return pl.ds(pl.multiple_of(which * width, LANES), width)

    loads = [load(i, src.at[:, columns(which, w)], dst) for i, (src, which, w, dst) in enumerate((
        (k_hbm, far, QW, k_far), (v_hbm, far, VW, v_far),
        (k_hbm, core, QW, kx.at[core, 128:384, :]), (v_hbm, core, VW, vx.at[core, 128:384, :]),
        (q_hbm, far, QW, q_far), (do_hbm, far, VW, do_far),
        (q_hbm, core, QW, q_own), (do_hbm, core, VW, do_own)))]
    loads.append(load(8, gain_hbm, gain_in))

    def remote(src, dst, ssem, rsem, to):
        return pltpu.make_async_remote_copy(
            src_ref=src, dst_ref=dst, send_sem=ssem, recv_sem=rsem,
            device_id={"seq": to}, device_id_type=pl.DeviceIdType.MESH)

    def chunk(ref, i):
        return ref.at[pl.ds(pl.multiple_of(i * rows, 16), rows), :]

    def cut(which, width):
        return pl.ds(pl.multiple_of(which * width, LANES), width)

    def pair_copy(index, src, dst):
        return remote(src, dst, pair_send.at[index], pair_recv.at[index], other)

    def is_in(span):
        return (chip >= span[0]) & (chip < span[1])

    def over(span, reach, body):
        lo, hi = span

        @pl.loop(lo, hi)
        def _(step):
            j = jnp.where(chip >= planes, step, lo + hi - 1 - step)

            @pl.when(j != chip)
            def _():
                body(j)

    def gather_copy(phase, src, dst, j):
        return remote(chunk(src, j), chunk(dst, chip), send_sem.at[phase, j], recv_sem.at[phase, chip], j * 2 + core)

    def gather_start(phase, span, src, dst):
        @pl.when(is_in(span))
        def _():
            over((0, chips), None, lambda j: gather_copy(phase, src, dst, j).start())

        chunk(dst, chip)[...] = chunk(src, chip)[...]

    def gather_wait(phase, span, src, dst):
        over(span, None, lambda j: remote(
            chunk(src, j), chunk(dst, j), send_sem.at[phase, j], recv_sem.at[phase, j], j * 2 + core).wait_recv())

        @pl.when(is_in(span))
        def _():
            over((0, chips), None, lambda j: gather_copy(phase, src, dst, j).wait_send())

    def spread_copy(phase, src, dst, j):
        return remote(chunk(src, j // 2), chunk(dst, chip), send_sem.at[phase, j], recv_sem.at[phase, chip],
                      j * 2 + core)

    def spread_start(phase, span, src, dst):
        over(span, None, lambda j: spread_copy(phase, src, dst, j).start())

        @pl.when(is_in(span))
        def _():
            chunk(dst, chip)[...] = chunk(src, chip // 2)[...]

        @pl.when(jnp.logical_not(is_in(span)))
        def _():
            dst[...] = jnp.zeros_like(dst)

    def spread_wait(phase, span, src, dst):
        @pl.when(is_in(span))
        def _():
            over((0, chips), None, lambda j: remote(
                chunk(src, j // 2), chunk(dst, j), send_sem.at[phase, j], recv_sem.at[phase, j],
                j * 2 + core).wait_recv())

        over(span, None, lambda j: spread_copy(phase, src, dst, j).wait_send())

    def near_copy(index, src, dst, to):
        return remote(src.at[0:PACKED, :], dst, near_send.at[index], near_recv.at[index], to * 2 + core)

    def scan(src, dst, reverse):
        def step(i, total):
            p = planes - 1 - i if reverse else i
            chunk(dst, p)[...] = total.astype(BF16)
            return total + (chunk(src, 2 * p)[...].astype(F32) + chunk(src, 2 * p + 1)[...].astype(F32))

        total = lax.fori_loop(0, planes - 1, step, jnp.zeros((rows, LANES), F32))
        chunk(dst, 0 if reverse else planes - 1)[...] = total.astype(BF16)

    def chip_sum(src, dst):
        dst[0:PACKED, :] = (src[0].astype(F32) + src[1].astype(F32)).astype(BF16)
        if chips * rows > PACKED:
            dst[PACKED:, :] = jnp.zeros((chips * rows - PACKED, LANES), BF16)

    early, late = (0, chips - 2), (2, chips)
    first_chip = chip == 0
    end_chip = chip == chips - 1
    after = jnp.minimum(chip + 1, chips - 1)
    before = jnp.maximum(chip - 1, 0)

    kt_own = ktx.at[core, :, 128:384]
    vt_own = vtx.at[core, :, 128:384]
    loads[0].wait()
    turn(kt_o, k_far)
    loads[1].wait()
    turn(vt_o, v_far)
    stage_state(kt_o, vt_o, st_out)
    def number(b):
        stage_num(*(r.at[b] for r in (qt, num, kx, vtx)))

    pl.semaphore_wait(barrier, chips)

    state_copy = pair_copy(0, st_out, st2.at[core])
    state_copy.start()
    loads[2].wait()
    turn(kt_own, kx.at[core, 128:384, :])
    loads[3].wait()
    turn(vt_own, vx.at[core, 128:384, :])
    stage_state(kt_own, vt_own, st2.at[core])
    token_copies = [
        pair_copy(1, k_far, kx.at[core, 128:384, :]),
        pair_copy(2, v_far, vx.at[core, 128:384, :]),
        pair_copy(3, q_far, qx),
        pair_copy(4, do_far, dox),
    ]
    pair_copy(0, st_out, st2.at[far]).wait_recv()
    chip_sum(st2, sum1)
    gather_start(0, early, sum1, got1)

    @pl.when(odd == 0)
    def _():
        near_copy(0, sum1, near1, chip + 1).start()

    def rim_copies():
        return [remote(src.at[1, 320:384, :], src.at[0, 64:128, :], rim_send.at[m], rim_recv.at[m], after * 2 + core)
                for m, src in enumerate((kx, vx))]

    loads[4].wait()
    loads[5].wait()
    for copy in token_copies:
        copy.start()
    state_copy.wait_send()
    for copy in loads[6:]:
        copy.wait()
    turn(qt.at[core], q_own)
    turn(dot.at[core], do_own)
    kx[0, 0:64, :] = jnp.zeros((64, QW), BF16)
    vx[0, 0:64, :] = jnp.zeros((64, VW), BF16)

    @pl.when(first_chip)
    def _():
        kx[0, 64:128, :] = jnp.zeros((64, QW), BF16)
        vx[0, 64:128, :] = jnp.zeros((64, VW), BF16)

    for c in range(VW // LANES):
        row = gain_in[pl.ds(core * (VW // LANES) + c, 1), :]
        gain[c * LANES : (c + 1) * LANES, :] = jnp.broadcast_to(row, (LANES, LANES)).T
    number(core)
    for copy in token_copies:
        copy.wait_send()
    arrivals = [
        pair_copy(1, k_far, kx.at[far, 128:384, :]),
        pair_copy(2, v_far, vx.at[far, 128:384, :]),
        token_copies[2], token_copies[3],
    ]
    for copy in arrivals:
        copy.wait_recv()
    turn(ktx.at[far, :, 128:384], kx.at[far, 128:384, :])
    turn(vtx.at[far, :, 128:384], vx.at[far, 128:384, :])
    turn(qt.at[far], qx)
    turn(dot.at[far], dox)
    kx[1, 0:128, :] = kx[0, 256:384, :]
    vx[1, 0:128, :] = vx[0, 256:384, :]
    ktx[1, :, 0:128] = ktx[0, :, 256:384]
    vtx[1, :, 0:128] = vtx[0, :, 256:384]

    @pl.when(jnp.logical_not(end_chip))
    def _():
        for copy in rim_copies():
            copy.start()

    def window(b, lo, hi):
        stage_win(lo, hi, first_chip if b == 0 else None, *(r.at[b] for r in (
            qt, dot, win, dq, dk, dv, kx, vx, ktx, vtx)))

    number(far)
    gather_wait(0, early, sum1, got1)
    scan(got1, send2, False)
    spread_start(1, late, send2, base1)
    window(1, 0, 4)

    @pl.when(jnp.logical_not(first_chip))
    def _():
        for copy in rim_copies():
            copy.wait_recv()

    @pl.when(jnp.logical_not(end_chip))
    def _():
        for copy in rim_copies():
            copy.wait_send()

    turn(ktx.at[0, :, 0:128], kx.at[0, 0:128, :])
    turn(vtx.at[0, :, 0:128], vx.at[0, 0:128, :])
    window(0, 0, 2)

    @pl.when(odd == 1)
    def _():
        near_copy(0, sum1, near1, chip).wait_recv()

    @pl.when(odd == 0)
    def _():
        near_copy(0, sum1, near1, chip + 1).wait_send()
        near1[...] = jnp.zeros_like(near1)

    spread_wait(1, late, send2, base1)

    def bases(base, near, state, dst, order):
        total = base[0:PACKED, :].astype(F32) + near[...].astype(F32)
        dst[order[0]] = total.astype(BF16)
        dst[order[1]] = (total + state[order[0]].astype(F32)).astype(BF16)

    bases(base1, near1, st2, prefix, (0, 1))
    for b in range(2):
        stage_mix(*(r.at[b] for r in (prefix, qt, dot, num)), gain, dnum.at[b], dst2.at[b])

    chip_sum(dst2, sum3)
    gather_start(2, late, sum3, got3)

    @pl.when(odd == 1)
    def _():
        near_copy(1, sum3, near3, chip - 1).start()

    window(0, 2, 4)

    for ref, at, lo in ((dk, 0, 0), (dv, QW, QW)):
        size = ref.shape[1] // 2
        top = ref[0, 0:size, 0:128]
        rim_out[lo // 2 : lo // 2 + size, :] = (pltpu.roll(top, 64, 1) + ref[0, size : 2 * size, 0:128]).astype(BF16)

    def rim_back(to):
        return remote(rim_out, rim_in, rim_send.at[2], rim_recv.at[2], to * 2 + core)

    @pl.when(jnp.logical_not(first_chip))
    def _():
        rim_back(before).start()

    def back(b, lo, hi):
        stage_back(lo, hi, *(r.at[b] for r in (prefix, qt)), ktx.at[b, :, 128:384], kx.at[b, 128:384, :],
                   vx.at[b, 128:384, :], *(r.at[b] for r in (dnum, dqt, dkb, dvb)))

    back(0, 0, 1)
    gather_wait(2, late, sum3, got3)
    scan(got3, send4, True)
    spread_start(3, early, send4, base3)
    turn_sum(out_o, num.at[far], win.at[far])
    out_copy = pair_copy(5, out_o, out_ref.at[:, cut(core, VW)])
    out_copy.start()
    turn_sum(out_ref.at[:, cut(core, VW)], num.at[core], win.at[core])
    back(0, 1, 2)
    back(1, 0, 2)
    turn_sum(qg_o, dqt.at[far], dq.at[far])
    qg_copy = pair_copy(6, qg_o, qg_ref.at[:, cut(core, QW)])
    qg_copy.start()
    turn_sum(qg_ref.at[:, cut(core, QW)], dqt.at[core], dq.at[core])

    @pl.when(end_chip)
    def _():
        rim_in[...] = jnp.zeros_like(rim_in)

    @pl.when(jnp.logical_not(end_chip))
    def _():
        rim_back(after).wait_recv()

    @pl.when(jnp.logical_not(first_chip))
    def _():
        rim_back(before).wait_send()

    for ref, lo in ((dk, 0), (dv, QW)):
        size = ref.shape[1] // 2
        ref[0, :, 256:384] = ref[0, :, 256:384] + ref[1, :, 0:128]
        got = rim_in[lo // 2 : lo // 2 + size, :].astype(F32)
        upper = lax.broadcasted_iota(jnp.int32, got.shape, 1) >= 64
        zero = jnp.zeros_like(got)
        ref[1, 0:size, 256:384] = ref[1, 0:size, 256:384] + jnp.where(upper, pltpu.roll(got, 64, 1), zero)
        ref[1, size : 2 * size, 256:384] = ref[1, size : 2 * size, 256:384] + jnp.where(upper, got, zero)

    @pl.when(odd == 0)
    def _():
        near_copy(1, sum3, near3, chip).wait_recv()

    @pl.when(odd == 1)
    def _():
        near_copy(1, sum3, near3, chip - 1).wait_send()
        near3[...] = jnp.zeros_like(near3)

    spread_wait(3, early, send4, base3)
    bases(base3, near3, dst2, suffix, (1, 0))

    def last(b, dk_to, dv_to):
        stage_last(suffix.at[b], ktx.at[b, :, 128:384], vtx.at[b, :, 128:384],
                   dk.at[b, :, 128:384], dv.at[b, :, 128:384], dkb.at[b], dvb.at[b], dk_to, dv_to)

    last(far, dkt.at[0], dvt.at[0])
    turn_out(kg_o, dkt.at[0])
    turn_out(vg_o, dvt.at[0])
    ends = [pair_copy(7, kg_o, kg_ref.at[:, cut(core, QW)]), pair_copy(8, vg_o, vg_ref.at[:, cut(core, VW)])]
    for copy in ends:
        copy.start()
    last(core, dkt.at[1], dvt.at[1])
    turn_out(kg_ref.at[:, cut(core, QW)], dkt.at[1])
    turn_out(vg_ref.at[:, cut(core, VW)], dvt.at[1])
    returns = [
        pair_copy(5, out_o, out_ref.at[:, cut(far, VW)]), pair_copy(6, qg_o, qg_ref.at[:, cut(far, QW)]),
        pair_copy(7, kg_o, kg_ref.at[:, cut(far, QW)]), pair_copy(8, vg_o, vg_ref.at[:, cut(far, VW)]),
    ]
    for copy in returns:
        copy.wait_recv()
        copy.wait_send()


def turn_out(dst, src):
    for c in range(dst.shape[1] // LANES):
        cols = slice(c * LANES, (c + 1) * LANES)
        dst[:, cols] = src[cols, :].T.astype(BF16)


def turn_sum(dst, one, two):
    for c in range(dst.shape[1] // LANES):
        cols = slice(c * LANES, (c + 1) * LANES)
        dst[:, cols] = (one[cols, :] + two[cols, :]).astype(BF16).T


def finish(result, out_hbm, qg_hbm, kg_hbm, vg_hbm, sems):
    copies = [pltpu.make_async_copy(result.at[:, a:b], dst, sems.at[i])
              for i, ((a, b), dst) in enumerate(zip(SPANS, (out_hbm, qg_hbm, kg_hbm, vg_hbm)))]
    for copy in copies:
        copy.start()
    for copy in copies:
        copy.wait()


def on_device(q, k, v, do, gain):
    n = lax.axis_size("seq")
    chips = n // 2
    rows = -(-PACKED // (16 * chips)) * 16
    vm = pltpu.VMEM

    def both(*shape, dtype=BF16):
        return vm((2,) + shape, dtype)

    packed = vm((PACKED, LANES), BF16)
    ring = vm((chips * rows, LANES), BF16)
    small = vm((chips // 2 * rows, LANES), BF16)
    rim = vm(((QW + VW) // 2, LANES), BF16)
    result = pl.pallas_call(
        functools.partial(whole, n, rows),
        out_shape=pltpu.VMEM((BLK, SPANS[-1][1]), BF16),
        in_specs=[pl.BlockSpec(memory_space=pltpu.HBM)] * 5,
        out_specs=pl.BlockSpec(memory_space=vm),
        scratch_shapes=[
            vm((BLK, QW), BF16), vm((BLK, VW), BF16), vm((BLK, QW), BF16), vm((BLK, VW), BF16),
            vm((BLK, QW), BF16), vm((BLK, VW), BF16), vm((H * DV // LANES, LANES), F32),
            pltpu.SemaphoreType.DMA((9,)),
            vm((QW, BLK), BF16), vm((VW, BLK), BF16), packed,
            both(PACKED, LANES), ring, ring, small, ring, packed, both(PACKED, LANES),
            both(PACKED, LANES), ring, ring, small, ring, packed, both(PACKED, LANES),
            rim, rim, vm((BLK, QW), BF16), vm((BLK, VW), BF16),
            both(QW, BLK), both(VW, BLK), both(VW, BLK),
            both(VW, BLK, dtype=F32), both(VW, BLK, dtype=F32), both(QW, BLK, dtype=F32),
            both(QW, 384, dtype=F32), both(VW, 384, dtype=F32),
            both(QW, BLK, dtype=F32), both(VW, BLK, dtype=F32), both(QW, BLK, dtype=F32),
            both(384, QW), both(384, VW), both(QW, 384), both(VW, 384),
            vm((VW, LANES), F32),
            vm((BLK, VW), BF16), vm((BLK, QW), BF16), vm((BLK, QW), BF16), vm((BLK, VW), BF16),
            both(QW, BLK), both(VW, BLK),
            pltpu.SemaphoreType.DMA((4, chips)), pltpu.SemaphoreType.DMA((4, chips)),
            pltpu.SemaphoreType.DMA((2,)), pltpu.SemaphoreType.DMA((2,)),
            pltpu.SemaphoreType.DMA((9,)), pltpu.SemaphoreType.DMA((9,)),
            pltpu.SemaphoreType.DMA((3,)), pltpu.SemaphoreType.DMA((3,)),
        ],
        compiler_params=pltpu.CompilerParams(
            vmem_limit_bytes=24 * 1024 * 1024, collective_id=0, has_side_effects=True),
    )(*(pltpu.with_memory_space_constraint(x, pltpu.HBM)
        for x in (q, k, v, do, gain.reshape(H * DV // LANES, LANES))))
    return pl.pallas_call(
        finish,
        out_shape=[jax.ShapeDtypeStruct(x.shape, BF16) for x in (do, q, k, v)],
        in_specs=[pl.BlockSpec(memory_space=vm)],
        out_specs=[pl.BlockSpec(memory_space=pltpu.HBM)] * 4,
        scratch_shapes=[pltpu.SemaphoreType.DMA((4,))],
        compiler_params=pltpu.CompilerParams(vmem_limit_bytes=1024 * 1024),
    )(result)


def solution(mesh):
    split = P(("groups", "seq"), None)
    return jax.shard_map(
        on_device, mesh=mesh, in_specs=(split,) * 4 + (P(),), out_specs=(split,) * 4, check_vma=False
    )
```

```python
import functools

import jax
import jax.numpy as jnp
from jax import lax
from jax.experimental import pallas as pl
from jax.experimental.pallas import tpu as pltpu
from jax.sharding import PartitionSpec as P

H = 16
FD = 16
DV = 64
WIN = 64
BLK = 256
LANES = 128
HC = H // 2
QW = HC * FD
VW = HC * DV
PACKED = VW + VW // 4
QUAD = 0.17677669529663687
EPS = 1e-06
NEG = -1e30
SPANS = ((0, H * DV), (H * DV, H * (DV + FD)), (H * (DV + FD), H * (DV + 2 * FD)), (H * (DV + 2 * FD), H * 2 * (DV + FD)))
F32 = jnp.float32
BF16 = jnp.bfloat16

NN = (((1,), (0,)), ((), ()))
NT = (((1,), (1,)), ((), ()))
TN = (((0,), (0,)), ((), ()))


def mm(a, b, dims=NN):
    return lax.dot_general(a, b, dims, preferred_element_type=F32)


def features(x):
    parts = [x * x * QUAD]
    for d in range(1, 8):
        parts.append(x * pltpu.roll(x, FD - d, 0) * 0.25)
    parts.append(x[:8] * x[8:] * 0.25)
    row = lax.broadcasted_iota(jnp.int32, (8, x.shape[1]), 0)
    parts.append(jnp.where(row == 0, 1.0, 0.0).astype(F32))
    parts.append(x * 0.5)
    return jnp.concatenate(parts, axis=0).astype(BF16)


def features_back(g, x):
    dx = (2.0 * QUAD) * g[:FD] * x
    for d in range(1, 8):
        part = g[d * FD : (d + 1) * FD] * 0.25
        dx = dx + part * pltpu.roll(x, FD - d, 0) + pltpu.roll(part * x, d, 0)
    half = g[128:136] * 0.25
    dx = dx + jnp.concatenate([half * x[8:], half * x[:8]], axis=0)
    return dx + 0.5 * g[144:160]


def turn(dst, src):
    for c in range(src.shape[1] // LANES):
        cols = slice(c * LANES, (c + 1) * LANES)
        dst[cols, :] = src[:, cols].T


def put_state(buf, group, states):
    for i, st in enumerate(states):
        at = group * 256 + i * 64
        buf[at : at + 64, :] = st[:, :128].astype(BF16)
    rest = jnp.concatenate([st[:, 128:160] for st in states], axis=1)
    buf[VW + group * 64 : VW + group * 64 + 64, :] = rest.astype(BF16)


def get_state(buf, group, i):
    at = group * 256 + i * 64
    main = buf[at : at + 64, :]
    rest = buf[VW + group * 64 : VW + group * 64 + 64, :][:, i * 32 : (i + 1) * 32]
    return main, rest


def qk_rows(h):
    return pl.ds(pl.multiple_of(h * FD, FD), FD) if not isinstance(h, int) else slice(h * FD, (h + 1) * FD)


def v_rows(h):
    return pl.ds(pl.multiple_of(h * DV, DV), DV) if not isinstance(h, int) else slice(h * DV, (h + 1) * DV)


def head_mask(rows, width, which):
    row = lax.broadcasted_iota(jnp.int32, (128, rows), 0)
    return (row >= which * width) & (row < (which + 1) * width)


def tile_scores(kx, q_all, head):
    zero = jnp.zeros_like(q_all)
    picked = jnp.where(head_mask(q_all.shape[1], FD, head), q_all, zero)
    return mm(kx, picked) * 0.25


def kernel_mask():
    r = lax.broadcasted_iota(jnp.int32, (128, 128), 0)
    c = lax.broadcasted_iota(jnp.int32, (128, 128), 1)
    return r <= c


def stage_state(kt, vt, state):
    for group in range(HC // 4):
        states = []
        for i in range(4):
            h = group * 4 + i
            phi = features(kt[qk_rows(h), :].astype(F32))
            states.append(mm(vt[v_rows(h), :], phi, NT))
        put_state(state, group, states)


def masked_quads(full, below):
    zero = jnp.zeros((128, 128), F32)
    top = jnp.concatenate([jnp.where(below, full[:128, :128], 0.0), full[:128, 128:]], axis=1)
    low = jnp.concatenate([zero, jnp.where(below, full[128:, 128:], 0.0)], axis=1)
    return jnp.concatenate([top, low], axis=0).astype(BF16)


def stage_num(qt_ref, num_ref, kx, vtx):
    below = kernel_mask()

    @pl.loop(0, HC // 2)
    def _(pair):
        for i in range(2):
            h = pair * 2 + i
            s = tile_scores(kx[128:384, :], qt_ref[...], h)
            kern = masked_quads(1.0 + s + 0.5 * s * s, below)
            num_ref[v_rows(h), :] = mm(vtx[v_rows(h), 128:384], kern)


def stage_win(lo, hi, first, qt_ref, dot_ref, win_ref, dq_ref, dk_ref, dv_ref, kx, vx, ktx, vtx):
    r = lax.broadcasted_iota(jnp.int32, (192, 256), 0)
    c = lax.rem(lax.broadcasted_iota(jnp.int32, (192, 256), 1), 128)
    band = (r >= c + 1) & (r <= c + 64)
    band0 = band if first is None else band & (r >= jnp.where(first, 64, 0))
    halves = [head_mask(128, DV, i) for i in range(2)]

    @pl.loop(lo, hi)
    def _(pair):
        prow = pl.ds(pl.multiple_of(pair * LANES, LANES), LANES)
        dks = [[], []]
        dvs = [[], []]
        for j in range(2):
            cols = slice(j * 128, (j + 1) * 128)
            keys = slice(j * 128, j * 128 + 256)
            near = slice(j * 128 + 64, j * 128 + 256)
            q_all = qt_ref[:, cols]
            zero = jnp.zeros_like(q_all)
            picked = jnp.concatenate(
                [jnp.where(head_mask(LANES, FD, pair * 2 + i), q_all, zero) for i in range(2)], axis=1)
            s = mm(kx[near, :], picked) * 0.25
            sw = jnp.where(band0 if j == 0 else band, s, NEG)
            e = jnp.exp(sw - jnp.max(sw, axis=0, keepdims=True))
            p = e * (1.0 / jnp.sum(e, axis=0, keepdims=True))
            do_pair = dot_ref[prow, cols]
            do_both = jnp.concatenate([jnp.where(m, do_pair, jnp.zeros_like(do_pair)) for m in halves], axis=1)
            dw = mm(vx[near, prow], do_both)
            ds = p * (dw - jnp.sum(p * dw, axis=0, keepdims=True)) * 0.25
            pad = jnp.zeros((64, 256), BF16)
            ds = jnp.concatenate([pad, ds.astype(BF16)], axis=0)
            wide = jnp.concatenate([pad, p.astype(BF16)], axis=0)
            for i in range(2):
                h = pair * 2 + i
                ds_one = ds[:, i * 128 : (i + 1) * 128]
                wide_one = wide[:, i * 128 : (i + 1) * 128]
                win_ref[v_rows(h), cols] = mm(vtx[v_rows(h), keys], wide_one)
                dq_ref[qk_rows(h), cols] = mm(ktx[qk_rows(h), keys], ds_one)
                dks[i].append(mm(qt_ref[qk_rows(h), cols], ds_one, NT))
                dvs[i].append(mm(dot_ref[v_rows(h), cols], wide_one, NT))
        for i in range(2):
            h = pair * 2 + i
            for dst, rows, parts in ((dk_ref, qk_rows(h), dks[i]), (dv_ref, v_rows(h), dvs[i])):
                dst[rows, 0:128] = parts[0][:, :128]
                dst[rows, 128:256] = parts[0][:, 128:] + parts[1][:, :128]
                dst[rows, 256:384] = parts[1][:, 128:]


def stage_mix(prefix_ref, qt_ref, dot_ref, num_ref, gain_ref, dnum_ref, state_ref):
    for group in range(HC // 4):
        states = []
        for i in range(4):
            h = group * 4 + i
            phi = features(qt_ref[qk_rows(h), :].astype(F32))
            main, rest = get_state(prefix_ref, group, i)
            num = num_ref[v_rows(h), :] + mm(main, phi[:128]) + mm(rest, phi[128:])
            inv = lax.rsqrt(jnp.mean(num * num, axis=0, keepdims=True) + EPS)
            gain = jnp.concatenate([gain_ref[v_rows(h), :]] * 2, axis=1)
            unit = num * inv
            num_ref[v_rows(h), :] = unit * gain
            dg = dot_ref[v_rows(h), :].astype(F32) * gain
            dnum = inv * (dg - unit * jnp.mean(dg * unit, axis=0, keepdims=True))
            half = dnum.astype(BF16)
            dnum_ref[v_rows(h), :] = half
            states.append(mm(half, phi, NT))
        put_state(state_ref, group, states)


def stage_back(lo, hi, prefix_ref, qt_ref, kt_ref, k_ref, v_ref, dnum_ref, dqt, dkb, dvb):
    below = kernel_mask()

    @pl.loop(lo, hi)
    def _(group):
        for i in range(4):
            h = group * 4 + i
            pcol = pl.ds(pl.multiple_of((group * 2 + i // 2) * LANES, LANES), LANES)
            main = prefix_ref[v_rows(h), :]
            rest = prefix_ref[pl.ds(pl.multiple_of(VW + group * 64, 64), 64), :][:, i * 32 : (i + 1) * 32]
            dnum = dnum_ref[v_rows(h), :]
            dphi = jnp.concatenate([mm(main, dnum, TN), mm(rest, dnum, TN)], axis=0)
            dq = features_back(dphi, qt_ref[qk_rows(h), :].astype(F32))
            s = tile_scores(k_ref[...], qt_ref[...], h)
            dn_pair = dnum_ref[pcol, :]
            dn_one = jnp.where(head_mask(BLK, DV, i % 2), dn_pair, jnp.zeros_like(dn_pair))
            dkern = mm(v_ref[:, pcol], dn_one)
            kern = masked_quads(1.0 + s + 0.5 * s * s, below)
            ds = masked_quads(dkern * (0.25 + 0.25 * s), below)
            dqt[qk_rows(h), :] = dq + mm(kt_ref[qk_rows(h), :], ds)
            dkb[qk_rows(h), :] = mm(qt_ref[qk_rows(h), :], ds, NT)
            dvb[v_rows(h), :] = mm(dnum, kern, NT)


def stage_last(groups, suffix_ref, kt_ref, vt_ref, dk_in, dv_in, dkb, dvb, dkt, dvt):
    for group in groups:
        for i in range(4):
            h = group * 4 + i
            main, rest = get_state(suffix_ref, group, i)
            x = kt_ref[qk_rows(h), :].astype(F32)
            phi = features(x)
            vt = vt_ref[v_rows(h), :]
            dv = dv_in[v_rows(h), :] + dvb[v_rows(h), :] + mm(main, phi[:128]) + mm(rest, phi[128:])
            dphi = jnp.concatenate([mm(main, vt, TN), mm(rest, vt, TN)], axis=0)
            dk = dk_in[qk_rows(h), :] + dkb[qk_rows(h), :] + features_back(dphi, x)
            dkt[qk_rows(h), :] = dk.astype(BF16)
            dvt[v_rows(h), :] = dv.astype(BF16)


def whole(n, rows, q_hbm, k_hbm, v_hbm, do_hbm, gain_hbm, res,
          k_far, v_far, q_far, do_far, q_own, do_own, gain_in, load_sem,
          kt_o, vt_o, st_out, st2, sum1, got1, send2, base1, near1, prefix,
          dst2, sum3, got3, send4, base3, near3, suffix, rim_out, rim_in,
          qx, dox, qt, dot, dnum, num, win, dq, dk, dv, dkb, dvb, dqt, kx, vx, ktx, vtx, gain,
          out_o, qg_o, kg_o, vg_o, dkt, dvt,
          send_sem, recv_sem, near_send, near_recv, pair_send, pair_recv, rim_send, rim_recv):
    me = lax.axis_index("seq")
    out_ref, qg_ref, kg_ref, vg_ref = (res.at[:, a:b] for a, b in SPANS)
    chips = n // 2
    planes = chips // 2
    chip = me // 2
    core = lax.rem(me, 2)
    far = 1 - core
    other = chip * 2 + far
    odd = lax.rem(chip, 2)
    barrier = pltpu.get_barrier_semaphore()

    def greet(to):
        pl.semaphore_signal(barrier, inc=1, device_id={"seq": to}, device_id_type=pl.DeviceIdType.MESH)

    @pl.loop(0, chips)
    def _(step):
        j = jnp.where(chip >= planes, step, chips - 1 - step)

        @pl.when(j != chip)
        def _():
            greet(j * 2 + core)

    greet(other)

    def load(index, src, dst):
        copy = pltpu.make_async_copy(src, dst, load_sem.at[index])
        copy.start()
        return copy

    def columns(which, width):
        return pl.ds(pl.multiple_of(which * width, LANES), width)

    loads = [load(i, src.at[:, columns(which, w)], dst) for i, (src, which, w, dst) in enumerate((
        (k_hbm, far, QW, k_far), (v_hbm, far, VW, v_far),
        (k_hbm, core, QW, kx.at[core, 128:384, :]), (v_hbm, core, VW, vx.at[core, 128:384, :]),
        (q_hbm, far, QW, q_far), (do_hbm, far, VW, do_far),
        (q_hbm, core, QW, q_own), (do_hbm, core, VW, do_own)))]
    loads.append(load(8, gain_hbm, gain_in))

    def remote(src, dst, ssem, rsem, to):
        return pltpu.make_async_remote_copy(
            src_ref=src, dst_ref=dst, send_sem=ssem, recv_sem=rsem,
            device_id={"seq": to}, device_id_type=pl.DeviceIdType.MESH)

    def chunk(ref, i):
        return ref.at[pl.ds(pl.multiple_of(i * rows, 16), rows), :]

    def cut(which, width):
        return pl.ds(pl.multiple_of(which * width, LANES), width)

    def pair_copy(index, src, dst):
        return remote(src, dst, pair_send.at[index], pair_recv.at[index], other)

    def is_in(span):
        return (chip >= span[0]) & (chip < span[1])

    def over(span, reach, body):
        lo, hi = span

        @pl.loop(lo, hi)
        def _(step):
            j = jnp.where(chip >= planes, step, lo + hi - 1 - step)

            @pl.when(j != chip)
            def _():
                body(j)

    def gather_copy(phase, src, dst, j):
        return remote(chunk(src, j), chunk(dst, chip), send_sem.at[phase, j], recv_sem.at[phase, chip], j * 2 + core)

    def gather_start(phase, span, src, dst):
        @pl.when(is_in(span))
        def _():
            over((0, chips), None, lambda j: gather_copy(phase, src, dst, j).start())

        chunk(dst, chip)[...] = chunk(src, chip)[...]

    def gather_wait(phase, span, src, dst):
        over(span, None, lambda j: remote(
            chunk(src, j), chunk(dst, j), send_sem.at[phase, j], recv_sem.at[phase, j], j * 2 + core).wait_recv())

        @pl.when(is_in(span))
        def _():
            over((0, chips), None, lambda j: gather_copy(phase, src, dst, j).wait_send())

    def spread_copy(phase, src, dst, j):
        return remote(chunk(src, j // 2), chunk(dst, chip), send_sem.at[phase, j], recv_sem.at[phase, chip],
                      j * 2 + core)

    def spread_start(phase, span, src, dst):
        over(span, None, lambda j: spread_copy(phase, src, dst, j).start())

        @pl.when(is_in(span))
        def _():
            chunk(dst, chip)[...] = chunk(src, chip // 2)[...]

        @pl.when(jnp.logical_not(is_in(span)))
        def _():
            dst[...] = jnp.zeros_like(dst)

    def spread_wait(phase, span, src, dst):
        @pl.when(is_in(span))
        def _():
            over((0, chips), None, lambda j: remote(
                chunk(src, j // 2), chunk(dst, j), send_sem.at[phase, j], recv_sem.at[phase, j],
                j * 2 + core).wait_recv())

        over(span, None, lambda j: spread_copy(phase, src, dst, j).wait_send())

    def near_copy(index, src, dst, to):
        return remote(src.at[0:PACKED, :], dst, near_send.at[index], near_recv.at[index], to * 2 + core)

    def scan(src, dst, reverse):
        def step(i, total):
            p = planes - 1 - i if reverse else i
            chunk(dst, p)[...] = total.astype(BF16)
            return total + (chunk(src, 2 * p)[...].astype(F32) + chunk(src, 2 * p + 1)[...].astype(F32))

        total = lax.fori_loop(0, planes - 1, step, jnp.zeros((rows, LANES), F32))
        chunk(dst, 0 if reverse else planes - 1)[...] = total.astype(BF16)

    def chip_sum(src, dst):
        dst[0:PACKED, :] = (src[0].astype(F32) + src[1].astype(F32)).astype(BF16)
        if chips * rows > PACKED:
            dst[PACKED:, :] = jnp.zeros((chips * rows - PACKED, LANES), BF16)

    early, late = (0, chips - 2), (2, chips)
    first_chip = chip == 0
    end_chip = chip == chips - 1
    after = jnp.minimum(chip + 1, chips - 1)
    before = jnp.maximum(chip - 1, 0)

    kt_own = ktx.at[core, :, 128:384]
    vt_own = vtx.at[core, :, 128:384]
    loads[0].wait()
    turn(kt_o, k_far)
    loads[1].wait()
    turn(vt_o, v_far)
    stage_state(kt_o, vt_o, st_out)
    def number(b):
        stage_num(*(r.at[b] for r in (qt, num, kx, vtx)))

    pl.semaphore_wait(barrier, chips)

    state_copy = pair_copy(0, st_out, st2.at[core])
    state_copy.start()
    loads[2].wait()
    turn(kt_own, kx.at[core, 128:384, :])
    loads[3].wait()
    turn(vt_own, vx.at[core, 128:384, :])
    stage_state(kt_own, vt_own, st2.at[core])
    token_copies = [
        pair_copy(1, k_far, kx.at[core, 128:384, :]),
        pair_copy(2, v_far, vx.at[core, 128:384, :]),
        pair_copy(3, q_far, qx),
        pair_copy(4, do_far, dox),
    ]
    pair_copy(0, st_out, st2.at[far]).wait_recv()
    chip_sum(st2, sum1)
    gather_start(0, early, sum1, got1)

    @pl.when(odd == 0)
    def _():
        near_copy(0, sum1, near1, chip + 1).start()

    def rim_copies():
        return [remote(src.at[1, 320:384, :], src.at[0, 64:128, :], rim_send.at[m], rim_recv.at[m], after * 2 + core)
                for m, src in enumerate((kx, vx))]

    loads[4].wait()
    loads[5].wait()
    for copy in token_copies:
        copy.start()
    state_copy.wait_send()
    for copy in loads[6:]:
        copy.wait()
    turn(qt.at[core], q_own)
    turn(dot.at[core], do_own)
    kx[0, 0:64, :] = jnp.zeros((64, QW), BF16)
    vx[0, 0:64, :] = jnp.zeros((64, VW), BF16)

    @pl.when(first_chip)
    def _():
        kx[0, 64:128, :] = jnp.zeros((64, QW), BF16)
        vx[0, 64:128, :] = jnp.zeros((64, VW), BF16)

    for c in range(VW // LANES):
        row = gain_in[pl.ds(core * (VW // LANES) + c, 1), :]
        gain[c * LANES : (c + 1) * LANES, :] = jnp.broadcast_to(row, (LANES, LANES)).T
    number(core)
    for copy in token_copies:
        copy.wait_send()
    arrivals = [
        pair_copy(1, k_far, kx.at[far, 128:384, :]),
        pair_copy(2, v_far, vx.at[far, 128:384, :]),
        token_copies[2], token_copies[3],
    ]
    for copy in arrivals:
        copy.wait_recv()
    turn(ktx.at[far, :, 128:384], kx.at[far, 128:384, :])
    turn(vtx.at[far, :, 128:384], vx.at[far, 128:384, :])
    turn(qt.at[far], qx)
    turn(dot.at[far], dox)
    kx[1, 0:128, :] = kx[0, 256:384, :]
    vx[1, 0:128, :] = vx[0, 256:384, :]
    ktx[1, :, 0:128] = ktx[0, :, 256:384]
    vtx[1, :, 0:128] = vtx[0, :, 256:384]

    @pl.when(jnp.logical_not(end_chip))
    def _():
        for copy in rim_copies():
            copy.start()

    def window(b, lo, hi):
        stage_win(lo, hi, first_chip if b == 0 else None, *(r.at[b] for r in (
            qt, dot, win, dq, dk, dv, kx, vx, ktx, vtx)))

    number(far)
    gather_wait(0, early, sum1, got1)
    scan(got1, send2, False)
    spread_start(1, late, send2, base1)
    window(1, 0, 4)

    @pl.when(jnp.logical_not(first_chip))
    def _():
        for copy in rim_copies():
            copy.wait_recv()

    @pl.when(jnp.logical_not(end_chip))
    def _():
        for copy in rim_copies():
            copy.wait_send()

    turn(ktx.at[0, :, 0:128], kx.at[0, 0:128, :])
    turn(vtx.at[0, :, 0:128], vx.at[0, 0:128, :])
    window(0, 0, 2)

    @pl.when(odd == 1)
    def _():
        near_copy(0, sum1, near1, chip).wait_recv()

    @pl.when(odd == 0)
    def _():
        near_copy(0, sum1, near1, chip + 1).wait_send()
        near1[...] = jnp.zeros_like(near1)

    spread_wait(1, late, send2, base1)

    def bases(base, near, state, dst, order):
        total = base[0:PACKED, :].astype(F32) + near[...].astype(F32)
        dst[order[0]] = total.astype(BF16)
        dst[order[1]] = (total + state[order[0]].astype(F32)).astype(BF16)

    bases(base1, near1, st2, prefix, (0, 1))
    for b in range(2):
        stage_mix(*(r.at[b] for r in (prefix, qt, dot, num)), gain, dnum.at[b], dst2.at[b])

    chip_sum(dst2, sum3)
    gather_start(2, late, sum3, got3)

    @pl.when(odd == 1)
    def _():
        near_copy(1, sum3, near3, chip - 1).start()

    window(0, 2, 4)

    for ref, at, lo in ((dk, 0, 0), (dv, QW, QW)):
        size = ref.shape[1] // 2
        top = ref[0, 0:size, 0:128]
        rim_out[lo // 2 : lo // 2 + size, :] = (pltpu.roll(top, 64, 1) + ref[0, size : 2 * size, 0:128]).astype(BF16)

    def rim_back(to):
        return remote(rim_out, rim_in, rim_send.at[2], rim_recv.at[2], to * 2 + core)

    @pl.when(jnp.logical_not(first_chip))
    def _():
        rim_back(before).start()

    def back(b, lo, hi):
        stage_back(lo, hi, *(r.at[b] for r in (prefix, qt)), ktx.at[b, :, 128:384], kx.at[b, 128:384, :],
                   vx.at[b, 128:384, :], *(r.at[b] for r in (dnum, dqt, dkb, dvb)))

    back(0, 0, 1)
    gather_wait(2, late, sum3, got3)
    scan(got3, send4, True)
    spread_start(3, early, send4, base3)
    turn_sum(out_o, num.at[far], win.at[far])
    out_copy = pair_copy(5, out_o, out_ref.at[:, cut(core, VW)])
    out_copy.start()
    turn_sum(out_ref.at[:, cut(core, VW)], num.at[core], win.at[core])
    back(0, 1, 2)
    back(1, 0, 2)
    turn_sum(qg_o, dqt.at[far], dq.at[far])
    qg_copy = pair_copy(6, qg_o, qg_ref.at[:, cut(core, QW)])
    qg_copy.start()
    turn_sum(qg_ref.at[:, cut(core, QW)], dqt.at[core], dq.at[core])

    @pl.when(end_chip)
    def _():
        rim_in[...] = jnp.zeros_like(rim_in)

    @pl.when(jnp.logical_not(end_chip))
    def _():
        rim_back(after).wait_recv()

    @pl.when(jnp.logical_not(first_chip))
    def _():
        rim_back(before).wait_send()

    for ref, lo in ((dk, 0), (dv, QW)):
        size = ref.shape[1] // 2
        ref[0, :, 256:384] = ref[0, :, 256:384] + ref[1, :, 0:128]
        got = rim_in[lo // 2 : lo // 2 + size, :].astype(F32)
        upper = lax.broadcasted_iota(jnp.int32, got.shape, 1) >= 64
        zero = jnp.zeros_like(got)
        ref[1, 0:size, 256:384] = ref[1, 0:size, 256:384] + jnp.where(upper, pltpu.roll(got, 64, 1), zero)
        ref[1, size : 2 * size, 256:384] = ref[1, size : 2 * size, 256:384] + jnp.where(upper, got, zero)

    @pl.when(odd == 0)
    def _():
        near_copy(1, sum3, near3, chip).wait_recv()

    @pl.when(odd == 1)
    def _():
        near_copy(1, sum3, near3, chip - 1).wait_send()
        near3[...] = jnp.zeros_like(near3)

    spread_wait(3, early, send4, base3)
    bases(base3, near3, dst2, suffix, (1, 0))

    def last(b, dk_to, dv_to, groups=range(HC // 4)):
        stage_last(groups, suffix.at[b], ktx.at[b, :, 128:384], vtx.at[b, :, 128:384],
                   dk.at[b, :, 128:384], dv.at[b, :, 128:384], dkb.at[b], dvb.at[b], dk_to, dv_to)

    part = VW // 2

    def vg_copy(g, which):
        to = pl.ds(pl.multiple_of(which * VW + g * part, LANES), part)
        return pair_copy(8 + g, vg_o.at[:, g * part : (g + 1) * part], vg_ref.at[:, to])

    for g in range(2):
        last(far, dkt.at[0], dvt.at[0], (g,))
        turn_out(vg_o.at[:, g * part : (g + 1) * part], dvt.at[0, g * part : (g + 1) * part, :])
        vg_copy(g, core).start()
    turn_out(kg_o, dkt.at[0])
    pair_copy(7, kg_o, kg_ref.at[:, cut(core, QW)]).start()
    last(core, dkt.at[1], dvt.at[1])
    turn_out(kg_ref.at[:, cut(core, QW)], dkt.at[1])
    turn_out(vg_ref.at[:, cut(core, VW)], dvt.at[1])
    returns = [
        pair_copy(5, out_o, out_ref.at[:, cut(far, VW)]), pair_copy(6, qg_o, qg_ref.at[:, cut(far, QW)]),
        pair_copy(7, kg_o, kg_ref.at[:, cut(far, QW)]), vg_copy(0, far), vg_copy(1, far),
    ]
    for copy in returns:
        copy.wait_recv()
        copy.wait_send()


def turn_out(dst, src):
    for c in range(dst.shape[1] // LANES):
        cols = slice(c * LANES, (c + 1) * LANES)
        dst[:, cols] = src[cols, :].T.astype(BF16)


def turn_sum(dst, one, two):
    for c in range(dst.shape[1] // LANES):
        cols = slice(c * LANES, (c + 1) * LANES)
        dst[:, cols] = (one[cols, :] + two[cols, :]).astype(BF16).T


def finish(result, out_hbm, qg_hbm, kg_hbm, vg_hbm, sems):
    copies = [pltpu.make_async_copy(result.at[:, a:b], dst, sems.at[i])
              for i, ((a, b), dst) in enumerate(zip(SPANS, (out_hbm, qg_hbm, kg_hbm, vg_hbm)))]
    for copy in copies:
        copy.start()
    for copy in copies:
        copy.wait()


def on_device(q, k, v, do, gain):
    n = lax.axis_size("seq")
    chips = n // 2
    rows = -(-PACKED // (16 * chips)) * 16
    vm = pltpu.VMEM

    def both(*shape, dtype=BF16):
        return vm((2,) + shape, dtype)

    packed = vm((PACKED, LANES), BF16)
    ring = vm((chips * rows, LANES), BF16)
    small = vm((chips // 2 * rows, LANES), BF16)
    rim = vm(((QW + VW) // 2, LANES), BF16)
    result = pl.pallas_call(
        functools.partial(whole, n, rows),
        out_shape=pltpu.VMEM((BLK, SPANS[-1][1]), BF16),
        in_specs=[pl.BlockSpec(memory_space=pltpu.HBM)] * 5,
        out_specs=pl.BlockSpec(memory_space=vm),
        scratch_shapes=[
            vm((BLK, QW), BF16), vm((BLK, VW), BF16), vm((BLK, QW), BF16), vm((BLK, VW), BF16),
            vm((BLK, QW), BF16), vm((BLK, VW), BF16), vm((H * DV // LANES, LANES), F32),
            pltpu.SemaphoreType.DMA((9,)),
            vm((QW, BLK), BF16), vm((VW, BLK), BF16), packed,
            both(PACKED, LANES), ring, ring, small, ring, packed, both(PACKED, LANES),
            both(PACKED, LANES), ring, ring, small, ring, packed, both(PACKED, LANES),
            rim, rim, vm((BLK, QW), BF16), vm((BLK, VW), BF16),
            both(QW, BLK), both(VW, BLK), both(VW, BLK),
            both(VW, BLK, dtype=F32), both(VW, BLK, dtype=F32), both(QW, BLK, dtype=F32),
            both(QW, 384, dtype=F32), both(VW, 384, dtype=F32),
            both(QW, BLK, dtype=F32), both(VW, BLK, dtype=F32), both(QW, BLK, dtype=F32),
            both(384, QW), both(384, VW), both(QW, 384), both(VW, 384),
            vm((VW, LANES), F32),
            vm((BLK, VW), BF16), vm((BLK, QW), BF16), vm((BLK, QW), BF16), vm((BLK, VW), BF16),
            both(QW, BLK), both(VW, BLK),
            pltpu.SemaphoreType.DMA((4, chips)), pltpu.SemaphoreType.DMA((4, chips)),
            pltpu.SemaphoreType.DMA((2,)), pltpu.SemaphoreType.DMA((2,)),
            pltpu.SemaphoreType.DMA((10,)), pltpu.SemaphoreType.DMA((10,)),
            pltpu.SemaphoreType.DMA((3,)), pltpu.SemaphoreType.DMA((3,)),
        ],
        compiler_params=pltpu.CompilerParams(
            vmem_limit_bytes=24 * 1024 * 1024, collective_id=0, has_side_effects=True),
    )(*(pltpu.with_memory_space_constraint(x, pltpu.HBM)
        for x in (q, k, v, do, gain.reshape(H * DV // LANES, LANES))))
    return pl.pallas_call(
        finish,
        out_shape=[jax.ShapeDtypeStruct(x.shape, BF16) for x in (do, q, k, v)],
        in_specs=[pl.BlockSpec(memory_space=vm)],
        out_specs=[pl.BlockSpec(memory_space=pltpu.HBM)] * 4,
        scratch_shapes=[pltpu.SemaphoreType.DMA((4,))],
        compiler_params=pltpu.CompilerParams(vmem_limit_bytes=1024 * 1024),
    )(result)


def solution(mesh):
    split = P(("groups", "seq"), None)
    return jax.shard_map(
        on_device, mesh=mesh, in_specs=(split,) * 4 + (P(),), out_specs=(split,) * 4, check_vma=False
    )
```

```python
import functools

import jax
import jax.numpy as jnp
from jax import lax
from jax.experimental import pallas as pl
from jax.experimental.pallas import tpu as pltpu
from jax.sharding import PartitionSpec as P

H = 16
FD = 16
DV = 64
WIN = 64
BLK = 256
LANES = 128
HC = H // 2
QW = HC * FD
VW = HC * DV
PACKED = VW + VW // 4
QUAD = 0.17677669529663687
EPS = 1e-06
NEG = -1e30
SPANS = ((0, H * DV), (H * DV, H * (DV + FD)), (H * (DV + FD), H * (DV + 2 * FD)), (H * (DV + 2 * FD), H * 2 * (DV + FD)))
F32 = jnp.float32
BF16 = jnp.bfloat16

NN = (((1,), (0,)), ((), ()))
NT = (((1,), (1,)), ((), ()))
TN = (((0,), (0,)), ((), ()))


def mm(a, b, dims=NN):
    return lax.dot_general(a, b, dims, preferred_element_type=F32)


def features(x):
    parts = [x * x * QUAD]
    for d in range(1, 8):
        parts.append(x * pltpu.roll(x, FD - d, 0) * 0.25)
    parts.append(x[:8] * x[8:] * 0.25)
    row = lax.broadcasted_iota(jnp.int32, (8, x.shape[1]), 0)
    parts.append(jnp.where(row == 0, 1.0, 0.0).astype(F32))
    parts.append(x * 0.5)
    return jnp.concatenate(parts, axis=0).astype(BF16)


def features_back(g, x):
    dx = (2.0 * QUAD) * g[:FD] * x
    for d in range(1, 8):
        part = g[d * FD : (d + 1) * FD] * 0.25
        dx = dx + part * pltpu.roll(x, FD - d, 0) + pltpu.roll(part * x, d, 0)
    half = g[128:136] * 0.25
    dx = dx + jnp.concatenate([half * x[8:], half * x[:8]], axis=0)
    return dx + 0.5 * g[144:160]


def turn(dst, src):
    for c in range(src.shape[1] // LANES):
        cols = slice(c * LANES, (c + 1) * LANES)
        dst[cols, :] = src[:, cols].T


def put_state(buf, group, states):
    for i, st in enumerate(states):
        at = group * 256 + i * 64
        buf[at : at + 64, :] = st[:, :128].astype(BF16)
    rest = jnp.concatenate([st[:, 128:160] for st in states], axis=1)
    buf[VW + group * 64 : VW + group * 64 + 64, :] = rest.astype(BF16)


def get_state(buf, group, i):
    at = group * 256 + i * 64
    main = buf[at : at + 64, :]
    rest = buf[VW + group * 64 : VW + group * 64 + 64, :][:, i * 32 : (i + 1) * 32]
    return main, rest


def qk_rows(h):
    return pl.ds(pl.multiple_of(h * FD, FD), FD) if not isinstance(h, int) else slice(h * FD, (h + 1) * FD)


def v_rows(h):
    return pl.ds(pl.multiple_of(h * DV, DV), DV) if not isinstance(h, int) else slice(h * DV, (h + 1) * DV)


def head_mask(rows, width, which):
    row = lax.broadcasted_iota(jnp.int32, (128, rows), 0)
    return (row >= which * width) & (row < (which + 1) * width)


def tile_scores(kx, q_all, head):
    zero = jnp.zeros_like(q_all)
    picked = jnp.where(head_mask(q_all.shape[1], FD, head), q_all, zero)
    return mm(kx, picked) * 0.25


def kernel_mask():
    r = lax.broadcasted_iota(jnp.int32, (128, 128), 0)
    c = lax.broadcasted_iota(jnp.int32, (128, 128), 1)
    return r <= c


def stage_state(kt, vt, state):
    for group in range(HC // 4):
        states = []
        for i in range(4):
            h = group * 4 + i
            phi = features(kt[qk_rows(h), :].astype(F32))
            states.append(mm(vt[v_rows(h), :], phi, NT))
        put_state(state, group, states)


def masked_quads(full, below):
    zero = jnp.zeros((128, 128), F32)
    top = jnp.concatenate([jnp.where(below, full[:128, :128], 0.0), full[:128, 128:]], axis=1)
    low = jnp.concatenate([zero, jnp.where(below, full[128:, 128:], 0.0)], axis=1)
    return jnp.concatenate([top, low], axis=0).astype(BF16)


def stage_num(qt_ref, num_ref, kx, vtx):
    below = kernel_mask()

    @pl.loop(0, HC // 2)
    def _(pair):
        for i in range(2):
            h = pair * 2 + i
            s = tile_scores(kx[128:384, :], qt_ref[...], h)
            kern = masked_quads(1.0 + s + 0.5 * s * s, below)
            num_ref[v_rows(h), :] = mm(vtx[v_rows(h), 128:384], kern)


def stage_win(lo, hi, first, qt_ref, dot_ref, win_ref, dq_ref, dk_ref, dv_ref, kx, vx, ktx, vtx):
    r = lax.broadcasted_iota(jnp.int32, (192, 256), 0)
    c = lax.rem(lax.broadcasted_iota(jnp.int32, (192, 256), 1), 128)
    band = (r >= c + 1) & (r <= c + 64)
    band0 = band if first is None else band & (r >= jnp.where(first, 64, 0))
    halves = [head_mask(128, DV, i) for i in range(2)]

    @pl.loop(lo, hi)
    def _(pair):
        prow = pl.ds(pl.multiple_of(pair * LANES, LANES), LANES)
        dks = [[], []]
        dvs = [[], []]
        for j in range(2):
            cols = slice(j * 128, (j + 1) * 128)
            keys = slice(j * 128, j * 128 + 256)
            near = slice(j * 128 + 64, j * 128 + 256)
            q_all = qt_ref[:, cols]
            zero = jnp.zeros_like(q_all)
            picked = jnp.concatenate(
                [jnp.where(head_mask(LANES, FD, pair * 2 + i), q_all, zero) for i in range(2)], axis=1)
            s = mm(kx[near, :], picked) * 0.25
            sw = jnp.where(band0 if j == 0 else band, s, NEG)
            e = jnp.exp(sw - jnp.max(sw, axis=0, keepdims=True))
            p = e * (1.0 / jnp.sum(e, axis=0, keepdims=True))
            do_pair = dot_ref[prow, cols]
            do_both = jnp.concatenate([jnp.where(m, do_pair, jnp.zeros_like(do_pair)) for m in halves], axis=1)
            dw = mm(vx[near, prow], do_both)
            ds = p * (dw - jnp.sum(p * dw, axis=0, keepdims=True)) * 0.25
            pad = jnp.zeros((64, 256), BF16)
            ds = jnp.concatenate([pad, ds.astype(BF16)], axis=0)
            wide = jnp.concatenate([pad, p.astype(BF16)], axis=0)
            for i in range(2):
                h = pair * 2 + i
                ds_one = ds[:, i * 128 : (i + 1) * 128]
                wide_one = wide[:, i * 128 : (i + 1) * 128]
                win_ref[v_rows(h), cols] = mm(vtx[v_rows(h), keys], wide_one)
                dq_ref[qk_rows(h), cols] = mm(ktx[qk_rows(h), keys], ds_one)
                dks[i].append(mm(qt_ref[qk_rows(h), cols], ds_one, NT))
                dvs[i].append(mm(dot_ref[v_rows(h), cols], wide_one, NT))
        for i in range(2):
            h = pair * 2 + i
            for dst, rows, parts in ((dk_ref, qk_rows(h), dks[i]), (dv_ref, v_rows(h), dvs[i])):
                dst[rows, 0:128] = parts[0][:, :128]
                dst[rows, 128:256] = parts[0][:, 128:] + parts[1][:, :128]
                dst[rows, 256:384] = parts[1][:, 128:]


def stage_mix(prefix_ref, qt_ref, dot_ref, num_ref, gain_ref, dnum_ref, state_ref):
    for group in range(HC // 4):
        states = []
        for i in range(4):
            h = group * 4 + i
            phi = features(qt_ref[qk_rows(h), :].astype(F32))
            main, rest = get_state(prefix_ref, group, i)
            num = num_ref[v_rows(h), :] + mm(main, phi[:128]) + mm(rest, phi[128:])
            inv = lax.rsqrt(jnp.mean(num * num, axis=0, keepdims=True) + EPS)
            gain = jnp.concatenate([gain_ref[v_rows(h), :]] * 2, axis=1)
            unit = num * inv
            num_ref[v_rows(h), :] = unit * gain
            dg = dot_ref[v_rows(h), :].astype(F32) * gain
            dnum = inv * (dg - unit * jnp.mean(dg * unit, axis=0, keepdims=True))
            half = dnum.astype(BF16)
            dnum_ref[v_rows(h), :] = half
            states.append(mm(half, phi, NT))
        put_state(state_ref, group, states)


def stage_back(lo, hi, prefix_ref, qt_ref, kt_ref, k_ref, v_ref, dnum_ref, dqt, dkb, dvb):
    below = kernel_mask()

    @pl.loop(lo, hi)
    def _(group):
        for i in range(4):
            h = group * 4 + i
            pcol = pl.ds(pl.multiple_of((group * 2 + i // 2) * LANES, LANES), LANES)
            main = prefix_ref[v_rows(h), :]
            rest = prefix_ref[pl.ds(pl.multiple_of(VW + group * 64, 64), 64), :][:, i * 32 : (i + 1) * 32]
            dnum = dnum_ref[v_rows(h), :]
            dphi = jnp.concatenate([mm(main, dnum, TN), mm(rest, dnum, TN)], axis=0)
            dq = features_back(dphi, qt_ref[qk_rows(h), :].astype(F32))
            s = tile_scores(k_ref[...], qt_ref[...], h)
            dn_pair = dnum_ref[pcol, :]
            dn_one = jnp.where(head_mask(BLK, DV, i % 2), dn_pair, jnp.zeros_like(dn_pair))
            dkern = mm(v_ref[:, pcol], dn_one)
            kern = masked_quads(1.0 + s + 0.5 * s * s, below)
            ds = masked_quads(dkern * (0.25 + 0.25 * s), below)
            dqt[qk_rows(h), :] = dq + mm(kt_ref[qk_rows(h), :], ds)
            dkb[qk_rows(h), :] = mm(qt_ref[qk_rows(h), :], ds, NT)
            dvb[v_rows(h), :] = mm(dnum, kern, NT)


def stage_last(groups, suffix_ref, kt_ref, vt_ref, dk_in, dv_in, dkb, dvb, dkt, dvt):
    for group in groups:
        for i in range(4):
            h = group * 4 + i
            main, rest = get_state(suffix_ref, group, i)
            x = kt_ref[qk_rows(h), :].astype(F32)
            phi = features(x)
            vt = vt_ref[v_rows(h), :]
            dv = dv_in[v_rows(h), :] + dvb[v_rows(h), :] + mm(main, phi[:128]) + mm(rest, phi[128:])
            dphi = jnp.concatenate([mm(main, vt, TN), mm(rest, vt, TN)], axis=0)
            dk = dk_in[qk_rows(h), :] + dkb[qk_rows(h), :] + features_back(dphi, x)
            dkt[qk_rows(h), :] = dk.astype(BF16)
            dvt[v_rows(h), :] = dv.astype(BF16)


def whole(n, rows, q_hbm, k_hbm, v_hbm, do_hbm, gain_hbm, res,
          k_far, v_far, q_far, do_far, q_own, do_own, gain_in, load_sem,
          kt_o, vt_o, st_out, st2, sum1, got1, send2, base1, near1, prefix,
          dst2, sum3, got3, send4, base3, near3, suffix, rim_out, rim_in,
          qx, dox, qt, dot, dnum, num, win, dq, dk, dv, dkb, dvb, dqt, kx, vx, ktx, vtx, gain,
          out_o, qg_o, kg_o, vg_o, dkt, dvt,
          send_sem, recv_sem, near_send, near_recv, pair_send, pair_recv, rim_send, rim_recv):
    me = lax.axis_index("seq")
    out_ref, qg_ref, kg_ref, vg_ref = (res.at[:, a:b] for a, b in SPANS)
    chips = n // 2
    planes = chips // 2
    chip = me // 2
    core = lax.rem(me, 2)
    far = 1 - core
    other = chip * 2 + far
    odd = lax.rem(chip, 2)
    barrier = pltpu.get_barrier_semaphore()

    def greet(to):
        pl.semaphore_signal(barrier, inc=1, device_id={"seq": to}, device_id_type=pl.DeviceIdType.MESH)

    @pl.loop(0, chips)
    def _(step):
        j = jnp.where(chip >= planes, step, chips - 1 - step)

        @pl.when(j != chip)
        def _():
            greet(j * 2 + core)

    greet(other)

    def load(index, src, dst):
        copy = pltpu.make_async_copy(src, dst, load_sem.at[index])
        copy.start()
        return copy

    def columns(which, width):
        return pl.ds(pl.multiple_of(which * width, LANES), width)

    loads = [load(i, src.at[:, columns(which, w)], dst) for i, (src, which, w, dst) in enumerate((
        (k_hbm, far, QW, k_far), (v_hbm, far, VW, v_far),
        (k_hbm, core, QW, kx.at[core, 128:384, :]), (v_hbm, core, VW, vx.at[core, 128:384, :]),
        (q_hbm, far, QW, q_far), (do_hbm, far, VW, do_far),
        (q_hbm, core, QW, q_own), (do_hbm, core, VW, do_own)))]
    loads.append(load(8, gain_hbm, gain_in))

    def remote(src, dst, ssem, rsem, to):
        return pltpu.make_async_remote_copy(
            src_ref=src, dst_ref=dst, send_sem=ssem, recv_sem=rsem,
            device_id={"seq": to}, device_id_type=pl.DeviceIdType.MESH)

    def chunk(ref, i):
        return ref.at[pl.ds(pl.multiple_of(i * rows, 16), rows), :]

    def cut(which, width):
        return pl.ds(pl.multiple_of(which * width, LANES), width)

    def pair_copy(index, src, dst):
        return remote(src, dst, pair_send.at[index], pair_recv.at[index], other)

    def is_in(span):
        return (chip >= span[0]) & (chip < span[1])

    def over(span, reach, body):
        lo, hi = span

        @pl.loop(lo, hi)
        def _(step):
            j = jnp.where(chip >= planes, step, lo + hi - 1 - step)

            @pl.when(j != chip)
            def _():
                body(j)

    def gather_copy(phase, src, dst, j):
        return remote(chunk(src, j), chunk(dst, chip), send_sem.at[phase, j], recv_sem.at[phase, chip], j * 2 + core)

    def gather_start(phase, span, src, dst):
        @pl.when(is_in(span))
        def _():
            over((0, chips), None, lambda j: gather_copy(phase, src, dst, j).start())

        chunk(dst, chip)[...] = chunk(src, chip)[...]

    def gather_wait(phase, span, src, dst):
        over(span, None, lambda j: remote(
            chunk(src, j), chunk(dst, j), send_sem.at[phase, j], recv_sem.at[phase, j], j * 2 + core).wait_recv())

        @pl.when(is_in(span))
        def _():
            over((0, chips), None, lambda j: gather_copy(phase, src, dst, j).wait_send())

    def spread_copy(phase, src, dst, j):
        return remote(chunk(src, j // 2), chunk(dst, chip), send_sem.at[phase, j], recv_sem.at[phase, chip],
                      j * 2 + core)

    def spread_start(phase, span, src, dst):
        over(span, None, lambda j: spread_copy(phase, src, dst, j).start())

        @pl.when(is_in(span))
        def _():
            chunk(dst, chip)[...] = chunk(src, chip // 2)[...]

        @pl.when(jnp.logical_not(is_in(span)))
        def _():
            dst[...] = jnp.zeros_like(dst)

    def spread_wait(phase, span, src, dst):
        @pl.when(is_in(span))
        def _():
            over((0, chips), None, lambda j: remote(
                chunk(src, j // 2), chunk(dst, j), send_sem.at[phase, j], recv_sem.at[phase, j],
                j * 2 + core).wait_recv())

        over(span, None, lambda j: spread_copy(phase, src, dst, j).wait_send())

    def near_copy(index, src, dst, to):
        return remote(src.at[0:PACKED, :], dst, near_send.at[index], near_recv.at[index], to * 2 + core)

    def scan(src, dst, reverse):
        def step(i, total):
            p = planes - 1 - i if reverse else i
            chunk(dst, p)[...] = total.astype(BF16)
            return total + (chunk(src, 2 * p)[...].astype(F32) + chunk(src, 2 * p + 1)[...].astype(F32))

        total = lax.fori_loop(0, planes - 1, step, jnp.zeros((rows, LANES), F32))
        chunk(dst, 0 if reverse else planes - 1)[...] = total.astype(BF16)

    def chip_sum(src, dst):
        dst[0:PACKED, :] = (src[0].astype(F32) + src[1].astype(F32)).astype(BF16)
        if chips * rows > PACKED:
            dst[PACKED:, :] = jnp.zeros((chips * rows - PACKED, LANES), BF16)

    early, late = (0, chips - 2), (2, chips)
    first_chip = chip == 0
    end_chip = chip == chips - 1
    after = jnp.minimum(chip + 1, chips - 1)
    before = jnp.maximum(chip - 1, 0)

    kt_own = ktx.at[core, :, 128:384]
    vt_own = vtx.at[core, :, 128:384]
    loads[0].wait()
    turn(kt_o, k_far)
    loads[1].wait()
    turn(vt_o, v_far)
    stage_state(kt_o, vt_o, st_out)
    def number(b):
        stage_num(*(r.at[b] for r in (qt, num, kx, vtx)))

    pl.semaphore_wait(barrier, chips)

    state_copy = pair_copy(0, st_out, st2.at[core])
    state_copy.start()
    loads[2].wait()
    turn(kt_own, kx.at[core, 128:384, :])
    loads[3].wait()
    turn(vt_own, vx.at[core, 128:384, :])
    stage_state(kt_own, vt_own, st2.at[core])
    token_copies = [
        pair_copy(1, k_far, kx.at[core, 128:384, :]),
        pair_copy(2, v_far, vx.at[core, 128:384, :]),
        pair_copy(3, q_far, qx),
        pair_copy(4, do_far, dox),
    ]
    pair_copy(0, st_out, st2.at[far]).wait_recv()
    chip_sum(st2, sum1)
    gather_start(0, early, sum1, got1)

    @pl.when(odd == 0)
    def _():
        near_copy(0, sum1, near1, chip + 1).start()

    def rim_copies():
        return [remote(src.at[1, 320:384, :], src.at[0, 64:128, :], rim_send.at[m], rim_recv.at[m], after * 2 + core)
                for m, src in enumerate((kx, vx))]

    loads[4].wait()
    loads[5].wait()
    for copy in token_copies:
        copy.start()
    state_copy.wait_send()
    for copy in loads[6:]:
        copy.wait()
    turn(qt.at[core], q_own)
    turn(dot.at[core], do_own)
    kx[0, 0:64, :] = jnp.zeros((64, QW), BF16)
    vx[0, 0:64, :] = jnp.zeros((64, VW), BF16)

    @pl.when(first_chip)
    def _():
        kx[0, 64:128, :] = jnp.zeros((64, QW), BF16)
        vx[0, 64:128, :] = jnp.zeros((64, VW), BF16)

    for c in range(VW // LANES):
        row = gain_in[pl.ds(core * (VW // LANES) + c, 1), :]
        gain[c * LANES : (c + 1) * LANES, :] = jnp.broadcast_to(row, (LANES, LANES)).T
    number(core)
    for copy in token_copies:
        copy.wait_send()
    arrivals = [
        pair_copy(1, k_far, kx.at[far, 128:384, :]),
        pair_copy(2, v_far, vx.at[far, 128:384, :]),
        token_copies[2], token_copies[3],
    ]
    for copy in arrivals:
        copy.wait_recv()
    turn(ktx.at[far, :, 128:384], kx.at[far, 128:384, :])
    turn(vtx.at[far, :, 128:384], vx.at[far, 128:384, :])
    turn(qt.at[far], qx)
    turn(dot.at[far], dox)
    kx[1, 0:128, :] = kx[0, 256:384, :]
    vx[1, 0:128, :] = vx[0, 256:384, :]
    ktx[1, :, 0:128] = ktx[0, :, 256:384]
    vtx[1, :, 0:128] = vtx[0, :, 256:384]

    @pl.when(jnp.logical_not(end_chip))
    def _():
        for copy in rim_copies():
            copy.start()

    def window(b, lo, hi):
        stage_win(lo, hi, first_chip if b == 0 else None, *(r.at[b] for r in (
            qt, dot, win, dq, dk, dv, kx, vx, ktx, vtx)))

    number(far)
    gather_wait(0, early, sum1, got1)
    scan(got1, send2, False)
    spread_start(1, late, send2, base1)
    window(1, 0, 4)

    @pl.when(jnp.logical_not(first_chip))
    def _():
        for copy in rim_copies():
            copy.wait_recv()

    @pl.when(jnp.logical_not(end_chip))
    def _():
        for copy in rim_copies():
            copy.wait_send()

    turn(ktx.at[0, :, 0:128], kx.at[0, 0:128, :])
    turn(vtx.at[0, :, 0:128], vx.at[0, 0:128, :])
    window(0, 0, 2)

    @pl.when(odd == 1)
    def _():
        near_copy(0, sum1, near1, chip).wait_recv()

    @pl.when(odd == 0)
    def _():
        near_copy(0, sum1, near1, chip + 1).wait_send()
        near1[...] = jnp.zeros_like(near1)

    spread_wait(1, late, send2, base1)

    def bases(base, near, state, dst, order):
        total = base[0:PACKED, :].astype(F32) + near[...].astype(F32)
        dst[order[0]] = total.astype(BF16)
        dst[order[1]] = (total + state[order[0]].astype(F32)).astype(BF16)

    bases(base1, near1, st2, prefix, (0, 1))
    for b in range(2):
        stage_mix(*(r.at[b] for r in (prefix, qt, dot, num)), gain, dnum.at[b], dst2.at[b])

    chip_sum(dst2, sum3)
    gather_start(2, late, sum3, got3)

    @pl.when(odd == 1)
    def _():
        near_copy(1, sum3, near3, chip - 1).start()

    window(0, 2, 4)

    for ref, at, lo in ((dk, 0, 0), (dv, QW, QW)):
        size = ref.shape[1] // 2
        top = ref[0, 0:size, 0:128]
        rim_out[lo // 2 : lo // 2 + size, :] = (pltpu.roll(top, 64, 1) + ref[0, size : 2 * size, 0:128]).astype(BF16)

    def rim_back(to):
        return remote(rim_out, rim_in, rim_send.at[2], rim_recv.at[2], to * 2 + core)

    @pl.when(jnp.logical_not(first_chip))
    def _():
        rim_back(before).start()

    def back(b, lo, hi):
        stage_back(lo, hi, *(r.at[b] for r in (prefix, qt)), ktx.at[b, :, 128:384], kx.at[b, 128:384, :],
                   vx.at[b, 128:384, :], *(r.at[b] for r in (dnum, dqt, dkb, dvb)))

    back(0, 0, 1)
    gather_wait(2, late, sum3, got3)
    scan(got3, send4, True)
    spread_start(3, early, send4, base3)
    turn_sum(out_o, num.at[far], win.at[far])
    out_copy = pair_copy(5, out_o, out_ref.at[:, cut(core, VW)])
    out_copy.start()
    turn_sum(out_ref.at[:, cut(core, VW)], num.at[core], win.at[core])
    back(0, 1, 2)
    back(1, 0, 2)
    turn_sum(qg_o, dqt.at[far], dq.at[far])
    qg_copy = pair_copy(6, qg_o, qg_ref.at[:, cut(core, QW)])
    qg_copy.start()
    turn_sum(qg_ref.at[:, cut(core, QW)], dqt.at[core], dq.at[core])

    @pl.when(end_chip)
    def _():
        rim_in[...] = jnp.zeros_like(rim_in)

    @pl.when(jnp.logical_not(end_chip))
    def _():
        rim_back(after).wait_recv()

    @pl.when(jnp.logical_not(first_chip))
    def _():
        rim_back(before).wait_send()

    for ref, lo in ((dk, 0), (dv, QW)):
        size = ref.shape[1] // 2
        ref[0, :, 256:384] = ref[0, :, 256:384] + ref[1, :, 0:128]
        got = rim_in[lo // 2 : lo // 2 + size, :].astype(F32)
        upper = lax.broadcasted_iota(jnp.int32, got.shape, 1) >= 64
        zero = jnp.zeros_like(got)
        ref[1, 0:size, 256:384] = ref[1, 0:size, 256:384] + jnp.where(upper, pltpu.roll(got, 64, 1), zero)
        ref[1, size : 2 * size, 256:384] = ref[1, size : 2 * size, 256:384] + jnp.where(upper, got, zero)

    @pl.when(odd == 0)
    def _():
        near_copy(1, sum3, near3, chip).wait_recv()

    @pl.when(odd == 1)
    def _():
        near_copy(1, sum3, near3, chip - 1).wait_send()
        near3[...] = jnp.zeros_like(near3)

    spread_wait(3, early, send4, base3)
    bases(base3, near3, dst2, suffix, (1, 0))

    def last(b, dk_to, dv_to, groups=range(HC // 4)):
        stage_last(groups, suffix.at[b], ktx.at[b, :, 128:384], vtx.at[b, :, 128:384],
                   dk.at[b, :, 128:384], dv.at[b, :, 128:384], dkb.at[b], dvb.at[b], dk_to, dv_to)

    part = VW // 2

    def vg_copy(g, which):
        to = pl.ds(pl.multiple_of(which * VW + g * part, LANES), part)
        return pair_copy(8 + g, vg_o.at[:, g * part : (g + 1) * part], vg_ref.at[:, to])

    for g in range(2):
        last(far, dkt.at[0], dvt.at[0], (g,))
        turn_out(vg_o.at[:, g * part : (g + 1) * part], dvt.at[0, g * part : (g + 1) * part, :])
        vg_copy(g, core).start()
    turn_out(kg_o, dkt.at[0])
    pair_copy(7, kg_o, kg_ref.at[:, cut(core, QW)]).start()
    last(core, dkt.at[1], dvt.at[1])
    turn_out(kg_ref.at[:, cut(core, QW)], dkt.at[1])
    turn_out(vg_ref.at[:, cut(core, VW)], dvt.at[1])
    returns = [
        pair_copy(5, out_o, out_ref.at[:, cut(far, VW)]), pair_copy(6, qg_o, qg_ref.at[:, cut(far, QW)]),
        pair_copy(7, kg_o, kg_ref.at[:, cut(far, QW)]), vg_copy(0, far), vg_copy(1, far),
    ]
    for copy in returns:
        copy.wait_recv()
        copy.wait_send()


def turn_out(dst, src):
    for c in range(dst.shape[1] // LANES):
        cols = slice(c * LANES, (c + 1) * LANES)
        dst[:, cols] = src[cols, :].T.astype(BF16)


def turn_sum(dst, one, two):
    for c in range(dst.shape[1] // LANES):
        cols = slice(c * LANES, (c + 1) * LANES)
        dst[:, cols] = (one[cols, :] + two[cols, :]).astype(BF16).T


def finish(result, out_hbm, qg_hbm, kg_hbm, vg_hbm, sems):
    half = BLK // 2
    copies = [pltpu.make_async_copy(result.at[r : r + half, a:b], dst.at[r : r + half, :], sems.at[i, r // half])
              for i, ((a, b), dst) in enumerate(zip(SPANS, (out_hbm, qg_hbm, kg_hbm, vg_hbm))) for r in (0, half)]
    for copy in copies:
        copy.start()
    for copy in copies:
        copy.wait()


def on_device(q, k, v, do, gain):
    n = lax.axis_size("seq")
    chips = n // 2
    rows = -(-PACKED // (16 * chips)) * 16
    vm = pltpu.VMEM

    def both(*shape, dtype=BF16):
        return vm((2,) + shape, dtype)

    packed = vm((PACKED, LANES), BF16)
    ring = vm((chips * rows, LANES), BF16)
    small = vm((chips // 2 * rows, LANES), BF16)
    rim = vm(((QW + VW) // 2, LANES), BF16)
    result = pl.pallas_call(
        functools.partial(whole, n, rows),
        out_shape=pltpu.VMEM((BLK, SPANS[-1][1]), BF16),
        in_specs=[pl.BlockSpec(memory_space=pltpu.HBM)] * 5,
        out_specs=pl.BlockSpec(memory_space=vm),
        scratch_shapes=[
            vm((BLK, QW), BF16), vm((BLK, VW), BF16), vm((BLK, QW), BF16), vm((BLK, VW), BF16),
            vm((BLK, QW), BF16), vm((BLK, VW), BF16), vm((H * DV // LANES, LANES), F32),
            pltpu.SemaphoreType.DMA((9,)),
            vm((QW, BLK), BF16), vm((VW, BLK), BF16), packed,
            both(PACKED, LANES), ring, ring, small, ring, packed, both(PACKED, LANES),
            both(PACKED, LANES), ring, ring, small, ring, packed, both(PACKED, LANES),
            rim, rim, vm((BLK, QW), BF16), vm((BLK, VW), BF16),
            both(QW, BLK), both(VW, BLK), both(VW, BLK),
            both(VW, BLK, dtype=F32), both(VW, BLK, dtype=F32), both(QW, BLK, dtype=F32),
            both(QW, 384, dtype=F32), both(VW, 384, dtype=F32),
            both(QW, BLK, dtype=F32), both(VW, BLK, dtype=F32), both(QW, BLK, dtype=F32),
            both(384, QW), both(384, VW), both(QW, 384), both(VW, 384),
            vm((VW, LANES), F32),
            vm((BLK, VW), BF16), vm((BLK, QW), BF16), vm((BLK, QW), BF16), vm((BLK, VW), BF16),
            both(QW, BLK), both(VW, BLK),
            pltpu.SemaphoreType.DMA((4, chips)), pltpu.SemaphoreType.DMA((4, chips)),
            pltpu.SemaphoreType.DMA((2,)), pltpu.SemaphoreType.DMA((2,)),
            pltpu.SemaphoreType.DMA((10,)), pltpu.SemaphoreType.DMA((10,)),
            pltpu.SemaphoreType.DMA((3,)), pltpu.SemaphoreType.DMA((3,)),
        ],
        compiler_params=pltpu.CompilerParams(
            vmem_limit_bytes=24 * 1024 * 1024, collective_id=0, has_side_effects=True),
    )(*(pltpu.with_memory_space_constraint(x, pltpu.HBM)
        for x in (q, k, v, do, gain.reshape(H * DV // LANES, LANES))))
    return pl.pallas_call(
        finish,
        out_shape=[jax.ShapeDtypeStruct(x.shape, BF16) for x in (do, q, k, v)],
        in_specs=[pl.BlockSpec(memory_space=vm)],
        out_specs=[pl.BlockSpec(memory_space=pltpu.HBM)] * 4,
        scratch_shapes=[pltpu.SemaphoreType.DMA((4, 2))],
        compiler_params=pltpu.CompilerParams(vmem_limit_bytes=1024 * 1024),
    )(result)


def solution(mesh):
    split = P(("groups", "seq"), None)
    return jax.shard_map(
        on_device, mesh=mesh, in_specs=(split,) * 4 + (P(),), out_specs=(split,) * 4, check_vma=False
    )
```
